32 devices in a mesh: dp: 8 (over y, x, core), seq: 4 (over z).
Axes of the slice: x: 2, y: 2, z: 4, core: 2. Of those that a mesh axis runs over, the one named last changes fastest.
Arguments:
- block_input: float32 [32, 200, 768], P(('dp', 'seq')), may hold values from -6 to 6
- norm1_gain: bfloat16 [768], P('dp'), may hold values from 0.5 to 1.5
- norm1_bias: bfloat16 [768], P('dp'), may hold values from -1 to 1
- qkv_weight: bfloat16 [768, 2304], P('dp'), may hold values from -0.21875 to 0.21875
- query_bias: bfloat16 [768], P('dp'), may hold values from -1 to 1
- value_bias: bfloat16 [768], P('dp'), may hold values from -1 to 1
- out_weight: bfloat16 [768, 768], P('dp'), may hold values from -0.875 to 0.875
- out_bias: bfloat16 [768], P('dp'), may hold values from -1 to 1
- norm2_gain: bfloat16 [768], P('dp'), may hold values from 0.5 to 1.5
- norm2_bias: bfloat16 [768], P('dp'), may hold values from -1 to 1
- router_weight: bfloat16 [768, 32], P('dp'), may hold values from -0.21875 to 0.21875
- gate_weight: bfloat16 [32, 768, 2048], P('dp', None, 'seq'), may hold values from -0.21875 to 0.21875
- up_weight: bfloat16 [32, 768, 2048], P('dp', None, 'seq'), may hold values from -0.21875 to 0.21875
- down_weight: bfloat16 [32, 2048, 768], P('dp', 'seq'), may hold values from -2 to 2
- routes: int32 [32, 200, 2], P(('dp', 'seq')), may hold values from 0 to 31, all different within a row; in each aligned block of 200 rows (0 to 199, 200 to 399, ..., all dimensions but the last counted through in order) at most 14 rows name the same one
- key_mask: int32 [32, 200], P('dp'), may hold values from 0 to 1, as said below
- cotangent: float32 [32, 200, 768], P(('dp', 'seq')), may hold values from -6 to 6
Outputs:
- block_output: float32 [32, 200, 768], P(('dp', 'seq'))
- input_grad: float32 [32, 200, 768], P(('dp', 'seq'))
- norm1_gain_grad: float32 [768], P('dp')
- norm1_bias_grad: float32 [768], P('dp')
- qkv_weight_grad: float32 [768, 2304], P('dp')
- query_bias_grad: float32 [768], P('dp')
- value_bias_grad: float32 [768], P('dp')
- out_weight_grad: float32 [768, 768], P('dp')
- out_bias_grad: float32 [768], P('dp')
- norm2_gain_grad: float32 [768], P('dp')
- norm2_bias_grad: float32 [768], P('dp')
- router_weight_grad: float32 [768, 32], P('dp')
- gate_weight_grad: float32 [32, 768, 2048], P('dp', None, 'seq')
- up_weight_grad: float32 [32, 768, 2048], P('dp', None, 'seq')
- down_weight_grad: float32 [32, 2048, 768], P('dp', 'seq')
The draws below stay inside these ranges and needn't reach their ends.
Inputs may be any that keep to these rules, and one draw needn't show every extreme that they name: `routes`: in each image, no expert is named by more than 14 tokens; a token's 2 experts differ. `key_mask`: each image has exactly 3 zeros, at positions that differ from image to image.
All inputs are finite; a program needn't handle non-finite values.
Results may differ from the reference program's by a relative error of at most 0.028.
Values may be sent and summed in bfloat16 or wider, within the bound.
No kernel may reach another device: no remote copies, remote signals or barrier semaphores. Data moves between devices by JAX's collectives and lax.ppermute only.
A program may use at most 192 MiB of HBM per device.

```python
import math
import jax
import jax.numpy as jnp
import numpy as np
from jax import lax

D = 768
HEADS = 12
HEAD = 64
EXPERTS = 32
FF = 2048
TOP = 2
LEN = 200
PADS = 3
CAP = 14
IMAGES = 32
SPLIT = 1
PIECES = 32
FF_PIECE = 2048


def draw_key_mask(key, part):
    scores = jax.random.randint(key, (IMAGES, LEN), 0, 1 << 20)
    scores = scores * LEN + jnp.arange(LEN, dtype=jnp.int32)[None, :]
    ordering = jnp.argsort(scores, axis=1)
    ranking = jnp.argsort(ordering, axis=1)
    return (ranking >= PADS).astype(jnp.int32)


def steps_of(rng, shape, pieces, smallest, largest):
    def one(axis_at, blocks):
        draws = jax.random.uniform(jax.random.fold_in(jax.random.fold_in(rng, 6), axis_at), (blocks,), jnp.float32, smallest / len(pieces), largest / len(pieces))
        return jnp.repeat(jnp.exp(draws), shape[axis_at] // blocks).reshape((-1,) + (1,) * (len(shape) - axis_at - 1))

    factor_of = one(*pieces[0])
    for cut in pieces[1:]:
        factor_of = factor_of * one(*cut)
    return factor_of


def shared_out(own_key, own, number, rows, number_of, top, most, skew):
    sequence = jax.random.permutation(own_key, number_of)
    crowded, usual = portions_of(number_of, rows * top, most, skew, True), portions_of(number_of, rows * top, most, skew, False)
    places = jnp.arange(number_of)

    def named(lengths, rotation):
        used = int((lengths > 0).sum())
        fixed = max(1, used // 4)
        shifted = fixed + (places - fixed + rotation * (used - fixed)) % max(1, number_of - fixed)
        return jnp.zeros((number_of,), jnp.int32).at[sequence[jnp.where(places < fixed, places, shifted)]].set(jnp.asarray(lengths, jnp.int32))

    lengths = jnp.where(number % 4 == 0, named(crowded, number // 4), named(usual, number - number // 4 - 1))
    mixed = jax.random.permutation(jax.random.fold_in(own, 3), number_of)
    giver, taker = mixed[0:number_of // 2 * 2:2], mixed[1:number_of // 2 * 2:2]
    margin = jnp.minimum(lengths[giver] - 1, most - lengths[taker]) // 2
    margin = jnp.where((giver == sequence[0]) | (taker == sequence[0]) | (lengths[taker] == 0), 0, jnp.maximum(margin, 0))
    shifted = jax.random.randint(jax.random.fold_in(own, 4), (number_of // 2,), 0, 1 << 20) % (margin + 1)
    lengths = lengths.at[giver].add(-shifted).at[taker].add(shifted)
    labels = jnp.searchsorted(jnp.cumsum(lengths), jnp.arange(rows * top), side="right").astype(jnp.int32)
    table = labels.reshape(top, rows).T
    table = table[jax.random.permutation(jax.random.fold_in(own, 1), rows)]
    rotation = jax.random.randint(jax.random.fold_in(own, 2), (rows, 1), 0, top)
    return jnp.take_along_axis(table, (jnp.arange(top)[None, :] + rotation) % top, axis=1)


def portions_of(amount, total, bound, lean, full):
    loads = [(1 << 20) // math.isqrt(standing ** lean) + 1 for standing in range(1, amount + 1)]
    largest = bound if full else min(bound, max(-(-total // amount), total * loads[0] // sum(loads)))
    least = 1 if total - largest >= amount - 1 else 0
    holding, spare = [largest] + [least] * (amount - 1), total - largest - least * (amount - 1)
    while spare > 0:
        free = [i for i in range(1, amount) if holding[i] < largest] or [i for i in range(1, amount) if holding[i] < bound]
        whole, budget = sum([loads[i] for i in free]), spare
        for i in free:
            addition = min(bound - holding[i], max(1, budget * loads[i] // whole), spare)
            holding[i] = holding[i] + addition
            spare = spare - addition
    return np.array(holding)


def normal_values(key, extent, scale, reach, shards=(), kind=jnp.bfloat16):
    entries = jax.random.normal(key, extent, jnp.float32) * scale
    if len(shards) > 0:
        entries = steps_of(key, extent, shards, -0.22, 0.18) * entries
    return jnp.clip(entries, min=-reach, max=reach).astype(kind)


def setup_inputs(seed: int = 0) -> dict:
    seeds = jax.random.split(jax.random.key(seed), 18)
    block_input = normal_values(seeds[0], (IMAGES, LEN, D), 1.0, 6.0, ((0, 32),), jnp.float32)
    norm1_gain = jnp.clip(1.0 + 0.1 * jax.random.normal(seeds[1], (D,), jnp.float32), 0.5, 1.5).astype(jnp.bfloat16)
    norm1_bias = normal_values(seeds[2], (D,), 0.2, 1.0, ((0, 8),))
    qkv_weight = normal_values(seeds[3], (D, 3 * D), D ** -0.5, 0.21875, ((0, 8),))
    query_bias = normal_values(seeds[4], (D,), 0.2, 1.0, ((0, 8),))
    value_bias = normal_values(seeds[5], (D,), 0.2, 1.0, ((0, 8),))
    out_weight = normal_values(seeds[6], (D, D), (D // 16) ** -0.5, 0.875, ((0, 8),))
    out_bias = normal_values(seeds[7], (D,), 0.2, 1.0, ((0, 8),))
    norm2_gain = jnp.clip(1.0 + 0.1 * jax.random.normal(seeds[8], (D,), jnp.float32), 0.5, 1.5).astype(jnp.bfloat16)
    norm2_bias = normal_values(seeds[9], (D,), 0.2, 1.0, ((0, 8),))
    router_weight = normal_values(seeds[10], (D, EXPERTS), D ** -0.5, 0.21875, ((0, 8),))
    gate_weight = normal_values(seeds[11], (PIECES, D, FF_PIECE), D ** -0.5, 0.21875, ((0, 8), (2, 4)))
    up_weight = normal_values(seeds[12], (PIECES, D, FF_PIECE), D ** -0.5, 0.21875, ((0, 8), (2, 4)))
    down_weight = normal_values(seeds[13], (PIECES, FF_PIECE, D), (max(1, FF // 256)) ** -0.5, 2.0, ((0, 8), (1, 4)))
    routes_keys = jax.random.split(jax.random.fold_in(seeds[14], 1), IMAGES * LEN // LEN)
    routes_turns = jax.random.permutation(jax.random.fold_in(seeds[14], 3), IMAGES * LEN // LEN)
    routes = jax.vmap(lambda own, number: shared_out(jax.random.fold_in(seeds[14], 2), own, number, LEN, EXPERTS, TOP, CAP, 1))(routes_keys, routes_turns).reshape((IMAGES, LEN, TOP))
    key_mask = draw_key_mask(jax.random.fold_in(seeds[17], 71), 0)
    cotangent = normal_values(seeds[16], (IMAGES, LEN, D), 1.0, 6.0, ((0, 32),), jnp.float32)
    return {"block_input": block_input, "norm1_gain": norm1_gain, "norm1_bias": norm1_bias, "qkv_weight": qkv_weight, "query_bias": query_bias, "value_bias": value_bias, "out_weight": out_weight, "out_bias": out_bias, "norm2_gain": norm2_gain, "norm2_bias": norm2_bias, "router_weight": router_weight, "gate_weight": gate_weight, "up_weight": up_weight, "down_weight": down_weight, "routes": routes, "key_mask": key_mask, "cotangent": cotangent}


epsilon = 1e-06

def rounded(values):
    return lax.optimization_barrier(values.astype(jnp.bfloat16))

def normalize(values, norm_gain, norm_bias):
    average = lax.optimization_barrier(jnp.mean(values, axis=-1, keepdims=True))
    centred = values - average
    variance = lax.optimization_barrier(jnp.mean(centred * centred, axis=-1, keepdims=True))
    inverse = lax.rsqrt(variance + epsilon)
    unit_rows = centred * inverse
    scaled = unit_rows * norm_gain.astype(jnp.float32) + norm_bias.astype(jnp.float32)
    return (scaled, unit_rows, inverse)

def normalize_back(upstream, unit_rows, inverse, norm_gain):
    scaled = upstream * norm_gain.astype(jnp.float32)
    mean_term = lax.optimization_barrier(jnp.mean(scaled, axis=-1, keepdims=True))
    proj_term = lax.optimization_barrier(jnp.mean(scaled * unit_rows, axis=-1, keepdims=True))
    return inverse * (scaled - mean_term - unit_rows * proj_term)

def gelu_tanh(values):
    return jax.nn.gelu(values, approximate=True)

def attention_parts(image_rows, mask_row, params):
    norm1_gain, norm1_bias, qkv_weight, query_bias, value_bias = params
    normed, unit_rows, inverse = normalize(image_rows, norm1_gain, norm1_bias)
    normed = rounded(normed)
    projected = jnp.dot(normed, qkv_weight, preferred_element_type=jnp.float32)
    queries = rounded(projected[:, :D] + query_bias.astype(jnp.float32))
    key_rows = rounded(projected[:, D:2 * D])
    value_rows = rounded(projected[:, 2 * D:] + value_bias.astype(jnp.float32))
    head_q = queries.reshape(LEN, HEADS, HEAD).astype(jnp.float32)
    head_k = key_rows.reshape(LEN, HEADS, HEAD).astype(jnp.float32)
    head_v = value_rows.reshape(LEN, HEADS, HEAD).astype(jnp.float32)
    scores = jnp.einsum('qhd,khd->hqk', head_q, head_k, precision=lax.Precision.HIGHEST) * (1.0 / math.sqrt(HEAD))
    key_open = mask_row.astype(jnp.float32)
    log_total = jnp.log(lax.optimization_barrier(jnp.sum(jnp.exp(scores) * key_open[None, None, :], axis=-1)))
    probs = jnp.exp(scores - log_total[..., None]) * key_open[None, None, :]
    probs_b = rounded(probs)
    mixed = rounded(jnp.einsum('hqk,khd->qhd', probs_b.astype(jnp.float32), head_v, precision=lax.Precision.HIGHEST)).reshape(LEN, D)
    return (normed, unit_rows, inverse, head_q, head_k, head_v, probs, probs_b, mixed)

def reference(block_input, norm1_gain, norm1_bias, qkv_weight, query_bias, value_bias, out_weight, out_bias, norm2_gain, norm2_bias, router_weight, gate_weight, up_weight, down_weight, routes, key_mask, cotangent):
    front = (norm1_gain, norm1_bias, qkv_weight, query_bias, value_bias)

    def forward_image(packed):
        image_rows, mask_row = packed
        mixed = attention_parts(image_rows, mask_row, front)[-1]
        return image_rows + jnp.dot(mixed, out_weight, preferred_element_type=jnp.float32) + out_bias.astype(jnp.float32)
    residual_one = lax.map(forward_image, (block_input, key_mask))
    normed_two, unit_two, inverse_two = normalize(residual_one, norm2_gain, norm2_bias)
    normed_two = rounded(normed_two)
    block_count = IMAGES
    flat_rows = normed_two.reshape(IMAGES * LEN, D)
    logits = jnp.dot(flat_rows, router_weight, preferred_element_type=jnp.float32).reshape(IMAGES, LEN, EXPERTS)
    expert_ids = jnp.arange(EXPERTS, dtype=jnp.int32)
    route_hot = (routes[..., None] == expert_ids).astype(jnp.int32)
    route_float = route_hot.astype(jnp.float32)
    logit_exp = jnp.exp(logits)
    router_probs = logit_exp / lax.optimization_barrier(jnp.sum(logit_exp, axis=-1, keepdims=True))
    gate = lax.optimization_barrier(jnp.sum(route_float * router_probs[:, :, None, :], axis=-1))
    per_token = lax.optimization_barrier(jnp.sum(route_hot, axis=2))
    earlier = jnp.cumsum(per_token, axis=1) - per_token
    slots = lax.optimization_barrier(jnp.sum(route_hot * earlier[:, :, None, :], axis=-1))
    block_ids = jnp.broadcast_to(jnp.arange(IMAGES, dtype=jnp.int32)[:, None], (IMAGES, LEN))
    flat_index = (routes * (block_count * CAP) + block_ids[:, :, None] * CAP + slots).reshape(-1).astype(jnp.int32)
    slot_total = EXPERTS * block_count * CAP
    copies = jnp.broadcast_to(normed_two[:, :, None, :], (IMAGES, LEN, TOP, D)).reshape(-1, D)
    dispatch = jnp.zeros((slot_total, D), jnp.bfloat16).at[flat_index].set(copies).reshape(EXPERTS, block_count * CAP, D)
    piece_ids = jnp.arange(PIECES, dtype=jnp.int32)

    def expert_forward(piece):
        rows = dispatch[piece // SPLIT]
        gate_pre = jnp.dot(rows, gate_weight[piece], preferred_element_type=jnp.float32)
        up_pre = jnp.dot(rows, up_weight[piece], preferred_element_type=jnp.float32)
        hidden = (gelu_tanh(gate_pre) * up_pre).astype(jnp.bfloat16)
        return jnp.dot(hidden, down_weight[piece], preferred_element_type=jnp.float32).astype(jnp.bfloat16)
    piece_out = lax.map(expert_forward, piece_ids)
    summed_out = lax.optimization_barrier(jnp.sum(piece_out.reshape(EXPERTS, SPLIT, block_count * CAP, D).astype(jnp.float32), axis=1)).reshape(slot_total, D)
    expert_out = summed_out[flat_index].reshape(IMAGES, LEN, TOP, D)
    block_output = residual_one + lax.optimization_barrier(jnp.sum(gate[..., None] * expert_out, axis=2))
    gate_grad = lax.optimization_barrier(jnp.sum(cotangent[:, :, None, :] * expert_out, axis=-1))
    routed_grad = (gate[..., None] * cotangent[:, :, None, :]).astype(jnp.bfloat16).reshape(-1, D)
    dispatch_grad = jnp.zeros((slot_total, D), jnp.bfloat16).at[flat_index].set(routed_grad).reshape(EXPERTS, block_count * CAP, D)

    def expert_backward(piece):
        rows = dispatch[piece // SPLIT]
        rows_grad = dispatch_grad[piece // SPLIT]
        gate_pre = jnp.dot(rows, gate_weight[piece], preferred_element_type=jnp.float32)
        up_pre = jnp.dot(rows, up_weight[piece], preferred_element_type=jnp.float32)
        activated, gelu_back = jax.vjp(gelu_tanh, gate_pre)
        hidden = (activated * up_pre).astype(jnp.bfloat16)
        hidden_grad = jnp.dot(rows_grad, down_weight[piece].T, preferred_element_type=jnp.float32)
        down_grad = jnp.dot(hidden.T, rows_grad, preferred_element_type=jnp.float32)
        gate_pre_grad = gelu_back(hidden_grad * up_pre)[0].astype(jnp.bfloat16)
        up_pre_grad = (hidden_grad * activated).astype(jnp.bfloat16)
        gate_grad_w = jnp.dot(rows.T, gate_pre_grad, preferred_element_type=jnp.float32)
        up_grad_w = jnp.dot(rows.T, up_pre_grad, preferred_element_type=jnp.float32)
        rows_back = (jnp.dot(gate_pre_grad, gate_weight[piece].T, preferred_element_type=jnp.float32) + jnp.dot(up_pre_grad, up_weight[piece].T, preferred_element_type=jnp.float32)).astype(jnp.bfloat16)
        return (rows_back, gate_grad_w, up_grad_w, down_grad)
    rows_back, gate_weight_grad, up_weight_grad, down_weight_grad = lax.map(expert_backward, piece_ids)
    summed_back = lax.optimization_barrier(jnp.sum(rows_back.reshape(EXPERTS, SPLIT, block_count * CAP, D).astype(jnp.float32), axis=1)).reshape(slot_total, D)
    moe_grad = lax.optimization_barrier(jnp.sum(summed_back[flat_index].reshape(IMAGES, LEN, TOP, D), axis=2))
    spread = lax.optimization_barrier(jnp.sum(route_float * gate_grad[..., None], axis=2))
    logit_grad = (router_probs * (spread - lax.optimization_barrier(jnp.sum(router_probs * spread, axis=-1, keepdims=True)))).astype(jnp.bfloat16)
    router_weight_grad = jnp.dot(flat_rows.T, logit_grad.reshape(IMAGES * LEN, EXPERTS), preferred_element_type=jnp.float32)
    normed_two_grad = moe_grad + jnp.dot(logit_grad, router_weight.T, preferred_element_type=jnp.float32)
    norm2_gain_grad = lax.optimization_barrier(jnp.sum(normed_two_grad * unit_two, axis=(0, 1)))
    norm2_bias_grad = lax.optimization_barrier(jnp.sum(normed_two_grad, axis=(0, 1)))
    residual_grad = cotangent + normalize_back(normed_two_grad, unit_two, inverse_two, norm2_gain)

    def backward_image(totals, packed):
        image_rows, mask_row, upstream = packed
        normed, unit_rows, inverse, head_q, head_k, head_v, probs, probs_b, mixed = attention_parts(image_rows, mask_row, front)
        upstream_b = upstream.astype(jnp.bfloat16)
        out_weight_part = jnp.dot(mixed.T, upstream_b, preferred_element_type=jnp.float32)
        out_bias_part = lax.optimization_barrier(jnp.sum(upstream, axis=0))
        mixed_grad = rounded(jnp.dot(upstream_b, out_weight.T, preferred_element_type=jnp.float32)).reshape(LEN, HEADS, HEAD).astype(jnp.float32)
        probs_grad = jnp.einsum('qhd,khd->hqk', mixed_grad, head_v, precision=lax.Precision.HIGHEST)
        row_term = lax.optimization_barrier(jnp.sum(probs * probs_grad, axis=-1, keepdims=True))
        score_grad = rounded(probs * (probs_grad - row_term) * (1.0 / math.sqrt(HEAD))).astype(jnp.float32)
        value_grad = jnp.einsum('hqk,qhd->khd', probs_b.astype(jnp.float32), mixed_grad, precision=lax.Precision.HIGHEST).astype(jnp.bfloat16).reshape(LEN, D)
        query_grad = jnp.einsum('hqk,khd->qhd', score_grad, head_k, precision=lax.Precision.HIGHEST).astype(jnp.bfloat16).reshape(LEN, D)
        key_grad = jnp.einsum('hqk,qhd->khd', score_grad, head_q, precision=lax.Precision.HIGHEST).astype(jnp.bfloat16).reshape(LEN, D)
        qkv_grad = jnp.concatenate([query_grad, key_grad, value_grad], axis=1)
        qkv_part = jnp.dot(normed.T, qkv_grad, preferred_element_type=jnp.float32)
        normed_grad = jnp.dot(qkv_grad, qkv_weight.T, preferred_element_type=jnp.float32)
        gain_part = lax.optimization_barrier(jnp.sum(normed_grad * unit_rows, axis=0))
        shift_part = lax.optimization_barrier(jnp.sum(normed_grad, axis=0))
        image_grad = upstream + normalize_back(normed_grad, unit_rows, inverse, norm1_gain)
        terms = (gain_part, shift_part, qkv_part, lax.optimization_barrier(jnp.sum(query_grad.astype(jnp.float32), axis=0)), lax.optimization_barrier(jnp.sum(value_grad.astype(jnp.float32), axis=0)), out_weight_part, out_bias_part)
        return (jax.tree.map(jnp.add, totals, terms), image_grad)
    zero_vec = jnp.zeros((D,), jnp.float32)
    start = (zero_vec, zero_vec, jnp.zeros((D, 3 * D), jnp.float32), zero_vec, zero_vec, jnp.zeros((D, D), jnp.float32), zero_vec)
    totals, input_grad = lax.scan(backward_image, start, (block_input, key_mask, residual_grad))
    norm1_gain_grad, norm1_bias_grad, qkv_weight_grad, query_bias_grad, value_bias_grad, out_weight_grad, out_bias_grad = totals
    return (block_output, input_grad, norm1_gain_grad, norm1_bias_grad, qkv_weight_grad, query_bias_grad, value_bias_grad, out_weight_grad, out_bias_grad, norm2_gain_grad, norm2_bias_grad, router_weight_grad, gate_weight_grad, up_weight_grad, down_weight_grad)
```

```python
import math

import jax
import jax.numpy as jnp
from jax import lax
from jax.sharding import PartitionSpec as P

HEAD = 64
EXPERTS = 32
TOP = 2
CAP = 14
CHUNKS = 2
LANES = 128


epsilon = 1e-06
f32 = jnp.float32
bf16 = jnp.bfloat16


def normalize(values, norm_gain, norm_bias):
    average = jnp.mean(values, axis=-1, keepdims=True)
    centred = values - average
    variance = jnp.mean(centred * centred, axis=-1, keepdims=True)
    inverse = lax.rsqrt(variance + epsilon)
    unit_rows = centred * inverse
    scaled = unit_rows * norm_gain + norm_bias
    return (scaled, unit_rows, inverse)


def normalize_back(upstream, unit_rows, inverse, norm_gain):
    scaled = upstream * norm_gain
    mean_term = jnp.mean(scaled, axis=-1, keepdims=True)
    proj_term = jnp.mean(scaled * unit_rows, axis=-1, keepdims=True)
    return inverse * (scaled - mean_term - unit_rows * proj_term)


def gelu_tanh(values):
    return jax.nn.gelu(values, approximate=True)


def dot(a, b, dims):
    return lax.dot_general(a, b, (dims, ((), ())), preferred_element_type=f32)


def partner(tensor, axis, flip):
    size = lax.axis_size(axis)
    return lax.ppermute(tensor, axis, [(i, i ^ flip) for i in range(size)])


def exchange(tensor, axis):
    return lax.all_to_all(tensor, axis, split_axis=0, concat_axis=0, tiled=False)


def spread_all(tensor, axis):
    size = lax.axis_size(axis)
    return exchange(jnp.broadcast_to(tensor[None], (size,) + tensor.shape), axis)


def bit_count(axis):
    return (lax.axis_size(axis) - 1).bit_length()


def split_columns(width):
    return (width // 2 // LANES) * LANES


def gather_rows(tensor):
    size = lax.axis_size("dp")
    bits = bit_count("dp")
    me = lax.axis_index("dp")
    rows, width = tensor.shape
    cut = split_columns(width)
    ordinary = list(range(1, bits))
    full = jnp.zeros((size, rows, width), tensor.dtype)
    for offset, half, order in (
        (0, tensor[:, :cut], ordinary),
        (cut, tensor[:, cut:], ordinary[::-1]),
    ):
        held, names = [half], [0]
        for bit in order + [0]:
            arrived = partner(jnp.stack(held), "dp", 1 << bit)
            held = held + [arrived[i] for i in range(len(names))]
            names = names + [name ^ (1 << bit) for name in names]
        for name, block in zip(names, held):
            full = lax.dynamic_update_slice(full, block[None], (me ^ name, 0, offset))
    return full


def place_of(model_width):
    size = lax.axis_size("dp")
    bits = bit_count("dp")
    rows = model_width // size
    feature = jnp.arange(model_width, dtype=jnp.int32)
    relative = (feature // rows) ^ lax.axis_index("dp")
    position = jnp.zeros_like(relative)
    for bit in range(bits):
        position = position + (((relative >> bit) & 1) << (bits - 1 - bit))
    return position * rows + feature % rows


def reduce_rows(blocks):
    size = lax.axis_size("dp")
    bits = bit_count("dp")
    width = blocks.shape[1]
    rows = blocks.shape[0] // size
    cut = split_columns(width)
    half_count = size // 2
    blocks = blocks.reshape(2, half_count * rows, width)
    total = blocks[0] + partner(blocks[1].astype(bf16), "dp", 1).astype(f32)
    total = total.reshape((2,) * (bits - 1) + (rows, width))
    ordinary = list(range(1, bits))
    parts = []
    for piece, order in (
        (total[..., :cut], ordinary),
        (total[..., cut:], ordinary[::-1]),
    ):
        left = list(ordinary)
        for bit in order:
            axis = left.index(bit)
            keep = lax.index_in_dim(piece, 0, axis, keepdims=False)
            send = lax.index_in_dim(piece, 1, axis, keepdims=False)
            piece = keep + partner(send.astype(bf16), "dp", 1 << bit).astype(f32)
            left.remove(bit)
        parts.append(piece)
    return jnp.concatenate(parts, axis=1)


def sum_groups(rows):
    groups = lax.axis_size("seq")
    count, width = rows.shape
    shares = exchange(rows.astype(bf16).reshape(groups, count // groups, width), "seq")
    total = jnp.sum(shares.astype(f32), axis=0).astype(bf16)
    return spread_all(total, "seq").reshape(count, width).astype(f32)


def per_device(
    block_input,
    norm1_gain,
    norm1_bias,
    qkv_weight,
    query_bias,
    value_bias,
    out_weight,
    out_bias,
    norm2_gain,
    norm2_bias,
    router_weight,
    gate_weight,
    up_weight,
    down_weight,
    routes,
    key_mask,
    cotangent,
):
    images, tokens, model_width = block_input.shape
    groups = lax.axis_size("seq")
    owners = lax.axis_size("dp")
    pieces = gate_weight.shape[0]
    split_count = owners * pieces // EXPERTS
    head_count = model_width // HEAD
    group_rows = groups * CAP
    me_seq = lax.axis_index("seq")
    me_dp = lax.axis_index("dp")
    inputs = block_input[0]
    upstream = cotangent[0]
    share = model_width // owners

    small = jnp.concatenate(
        [
            jnp.stack(
                [norm1_gain, norm1_bias, query_bias, value_bias, out_bias, norm2_gain, norm2_bias]
            ),
            router_weight.T,
        ],
        axis=0,
    )
    small_all = spread_all(small, "dp")
    small_full = jnp.transpose(small_all, (1, 0, 2)).reshape(small.shape[0], model_width)
    vectors = small_full[:7].astype(f32)
    gain_one, shift_one, query_full, value_full, obias_full, gain_two, shift_two = [
        vectors[i] for i in range(7)
    ]
    router_rows = small_full[7:]
    qkv_full = gather_rows(qkv_weight).reshape(model_width, 3 * model_width)
    out_full = gather_rows(out_weight).reshape(model_width, model_width)

    expert_ids = jnp.arange(EXPERTS, dtype=jnp.int32)
    route_hot = routes[0][..., None] == expert_ids
    per_token = jnp.any(route_hot, axis=1)
    order_ids = jnp.arange(tokens, dtype=jnp.int32)
    before = (order_ids[:, None] > order_ids[None, :]).astype(bf16)
    earlier = dot(before, per_token.astype(bf16), ((1,), (0,)))
    slots = jnp.sum(jnp.where(route_hot, earlier[:, None, :], 0.0), axis=-1).astype(jnp.int32)
    target = routes[0] * group_rows + slots
    targets = jnp.stack(
        [target] + [partner(target, "seq", j) + j * CAP for j in range(1, groups)]
    ).reshape(groups * tokens, TOP)
    slot_ids = jnp.arange(EXPERTS * group_rows, dtype=jnp.int32)
    place = (
        (targets[:, 0:1] == slot_ids) | (targets[:, 1:2] == slot_ids)
    ).astype(bf16)

    def group_tokens(rows):
        return jnp.concatenate([rows] + [partner(rows, "seq", j) for j in range(1, groups)], axis=0)

    def to_owners(rows):
        width = rows.shape[1]
        filled = dot(place, group_tokens(rows), ((0,), (0,))).astype(bf16)
        filled = filled.reshape(EXPERTS, group_rows, width)
        filled = jnp.repeat(filled, split_count, axis=0) if split_count > 1 else filled
        arrived = exchange(filled.reshape(owners, pieces * group_rows, width), "dp")
        arrived = arrived.reshape(owners, pieces, group_rows, width)
        return jnp.transpose(arrived, (1, 0, 2, 3)).reshape(pieces, owners * group_rows, width)

    def to_sources(rows):
        width = rows.shape[-1]
        rows = rows.reshape(pieces, owners, group_rows, width)
        rows = jnp.transpose(rows, (1, 0, 2, 3)).reshape(owners, pieces * group_rows, width)
        returned = exchange(rows, "dp")
        return returned.reshape(EXPERTS, split_count, group_rows, width)

    def to_tokens(returned):
        width = returned.shape[-1]
        total = None
        for half_index in range(split_count):
            part = dot(
                place, returned[:, half_index].reshape(EXPERTS * group_rows, width), ((1,), (0,))
            )
            total = part if total is None else total + part
        return sum_tokens(total.reshape(groups, tokens, width), bf16)

    def sum_tokens(parts, kind):
        total = parts[0]
        for j in range(1, groups):
            total = total + partner(parts[j].astype(kind), "seq", j).astype(f32)
        return total

    cot_rows = to_owners(upstream.astype(bf16))

    normed_one, unit_one, inverse_one = normalize(inputs, gain_one, shift_one)
    normed_one = normed_one.astype(bf16)
    bias_row = jnp.concatenate([query_full, jnp.zeros((model_width,), f32), value_full])
    projected = (dot(qkv_full, normed_one, ((0,), (1,))) + bias_row[:, None]).astype(bf16)
    heads = projected.reshape(3, head_count, HEAD, tokens)
    head_q, head_k, head_v = heads[0], heads[1], heads[2]
    mask_rows = lax.dynamic_slice_in_dim(key_mask, me_seq * images, images, axis=0)
    key_open = mask_rows.astype(f32)[:, None, :]
    scale = 1.0 / math.sqrt(HEAD)
    scores = jnp.einsum("hdq,hdk->hqk", head_q, head_k, preferred_element_type=f32) * scale
    log_total = jnp.log(jnp.sum(jnp.exp(scores) * key_open, axis=-1, keepdims=True))
    probs = jnp.exp(scores - log_total) * key_open
    probs_b = probs.astype(bf16)
    mixed = jnp.einsum("hqk,hdk->hdq", probs_b, head_v, preferred_element_type=f32)
    mixed = mixed.astype(bf16).reshape(model_width, tokens)
    residual_one = inputs + dot(mixed, out_full, ((0,), (0,))) + obias_full
    normed_two, unit_two, inverse_two = normalize(residual_one, gain_two, shift_two)
    normed_two = normed_two.astype(bf16)

    chunk = model_width // CHUNKS
    spans = [slice(c * chunk, (c + 1) * chunk) for c in range(CHUNKS)]
    hidden_up = jnp.einsum("erd,efd->erf", cot_rows, down_weight, preferred_element_type=f32)
    row_chunks = [to_owners(normed_two[:, span]) for span in spans]
    gate_pre = up_pre = slot_logits = 0.0
    for rows, span in zip(row_chunks, spans):
        gate_pre = gate_pre + jnp.einsum(
            "erd,edf->erf", rows, gate_weight[:, span], preferred_element_type=f32
        )
        up_pre = up_pre + jnp.einsum(
            "erd,edf->erf", rows, up_weight[:, span], preferred_element_type=f32
        )
        slot_logits = slot_logits + jnp.einsum(
            "erd,nd->ern", rows, router_rows[:, span], preferred_element_type=f32
        )
    slot_exp = jnp.exp(slot_logits)
    piece_ids = me_dp * pieces + jnp.arange(pieces, dtype=jnp.int32)
    mine = (piece_ids // split_count)[:, None, None] == expert_ids
    slot_gate = jnp.sum(jnp.where(mine, slot_exp, 0.0), axis=-1, keepdims=True) / jnp.sum(
        slot_exp, axis=-1, keepdims=True
    )
    activated, gelu_back = jax.vjp(gelu_tanh, gate_pre)
    hidden = (activated * up_pre).astype(bf16)
    slot_score = jnp.sum(hidden.astype(f32) * hidden_up, axis=-1)
    hidden_grad = hidden_up * slot_gate
    gate_pre_grad = gelu_back(hidden_grad * up_pre)[0].astype(bf16)
    up_pre_grad = (hidden_grad * activated).astype(bf16)

    score_back = to_sources(slot_score[..., None])[..., 0]
    score_back = jnp.sum(score_back, axis=1).reshape(1, EXPERTS * group_rows)
    gate_parts = jnp.stack(
        [
            jnp.sum(jnp.where(targets[:, k : k + 1] == slot_ids, score_back, 0.0), axis=-1)
            for k in range(TOP)
        ],
        axis=-1,
    ).reshape(groups, tokens, TOP)
    gate_grads = sum_tokens(gate_parts, f32)

    back_chunks = []
    for span in spans:
        rows_back = jnp.einsum(
            "erf,edf->erd", gate_pre_grad, gate_weight[:, span], preferred_element_type=f32
        ) + jnp.einsum("erf,edf->erd", up_pre_grad, up_weight[:, span], preferred_element_type=f32)
        back_chunks.append(to_sources(rows_back.astype(bf16)))
    moe_grad = jnp.concatenate([to_tokens(part) for part in back_chunks], axis=1)

    out_rows = jnp.einsum("erf,efd->erd", hidden, down_weight, preferred_element_type=f32)
    out_rows = (out_rows * slot_gate).astype(bf16)
    out_rows, back_chunks = lax.optimization_barrier((out_rows, back_chunks))
    out_tokens = jnp.concatenate(
        [to_tokens(to_sources(out_rows[..., span])) for span in spans], axis=1
    )
    block_output = residual_one + out_tokens

    rows_all = jnp.concatenate(row_chunks, axis=-1)
    rows_grad = (cot_rows.astype(f32) * slot_gate).astype(bf16)
    down_grad = jnp.einsum("erf,erd->efd", hidden, rows_grad, preferred_element_type=f32)
    gate_grad_w = jnp.einsum("erd,erf->edf", rows_all, gate_pre_grad, preferred_element_type=f32)
    up_grad_w = jnp.einsum("erd,erf->edf", rows_all, up_pre_grad, preferred_element_type=f32)

    logits = dot(normed_two, router_rows, ((1,), (1,)))
    logit_exp = jnp.exp(logits)
    router_probs = logit_exp / jnp.sum(logit_exp, axis=-1, keepdims=True)
    spread = jnp.sum(jnp.where(route_hot, gate_grads[..., None], 0.0), axis=1)
    logit_grad = (
        router_probs * (spread - jnp.sum(router_probs * spread, axis=-1, keepdims=True))
    ).astype(bf16)
    router_grad = dot(logit_grad, normed_two, ((0,), (0,)))
    normed_two_grad = moe_grad + dot(logit_grad, router_rows, ((1,), (0,)))
    gain_two_grad = jnp.sum(normed_two_grad * unit_two, axis=0)
    shift_two_grad = jnp.sum(normed_two_grad, axis=0)
    residual_grad = upstream + normalize_back(normed_two_grad, unit_two, inverse_two, gain_two)
    residual_b = residual_grad.astype(bf16)
    out_bias_grad = jnp.sum(residual_grad, axis=0)

    position = place_of(model_width)
    turn = (position[:, None] == jnp.arange(model_width, dtype=jnp.int32)).astype(bf16)

    def turned(rows):
        return lax.dot_general(
            turn, rows, (((0,), (1,)), ((), ())),
            precision=lax.Precision.HIGHEST, preferred_element_type=f32,
        )

    mixed_turned = dot(turn, mixed, ((0,), (0,))).astype(bf16)
    out_blocks = dot(mixed_turned, residual_b, ((1,), (0,)))
    small_two = jnp.concatenate(
        [gain_two_grad[None], shift_two_grad[None], out_bias_grad[None], router_grad], axis=0
    )
    small_two = jnp.pad(small_two, ((0, LANES - small_two.shape[0]), (0, 0)))
    sums_two = sum_groups(reduce_rows(jnp.concatenate([out_blocks, turned(small_two)], axis=1)))

    grad_heads = dot(out_full, residual_b, ((1,), (1,))).astype(bf16)
    grad_heads = grad_heads.reshape(head_count, HEAD, tokens)
    probs_grad = jnp.einsum("hdq,hdk->hqk", grad_heads, head_v, preferred_element_type=f32)
    row_term = jnp.sum(probs * probs_grad, axis=-1, keepdims=True)
    score_grad = (probs * (probs_grad - row_term) * scale).astype(bf16)
    value_grad = jnp.einsum(
        "hqk,hdq->hdk", probs_b, grad_heads, preferred_element_type=f32
    ).astype(bf16)
    query_grad = jnp.einsum(
        "hqk,hdk->hdq", score_grad, head_k, preferred_element_type=f32
    ).astype(bf16)
    key_grad = jnp.einsum(
        "hqk,hdq->hdk", score_grad, head_q, preferred_element_type=f32
    ).astype(bf16)
    qkv_grad = jnp.stack([query_grad, key_grad, value_grad]).reshape(3 * model_width, tokens)
    bias_grads = jnp.sum(qkv_grad.astype(f32), axis=1)
    normed_one_grad = dot(qkv_grad, qkv_full, ((0,), (1,)))
    gain_one_grad = jnp.sum(normed_one_grad * unit_one, axis=0)
    shift_one_grad = jnp.sum(normed_one_grad, axis=0)
    input_grad = residual_grad + normalize_back(normed_one_grad, unit_one, inverse_one, gain_one)

    normed_turned = dot(turn, normed_one, ((0,), (1,))).astype(bf16)
    qkv_blocks = dot(normed_turned, qkv_grad, ((1,), (1,)))
    small_one = jnp.stack(
        [gain_one_grad, shift_one_grad, bias_grads[:model_width], bias_grads[2 * model_width :]]
    )
    small_one = jnp.pad(small_one, ((0, LANES - small_one.shape[0]), (0, 0)))
    sums_one = sum_groups(reduce_rows(jnp.concatenate([qkv_blocks, turned(small_one)], axis=1)))

    base = 3 * model_width
    return (
        block_output[None],
        input_grad[None],
        sums_one[:, base],
        sums_one[:, base + 1],
        sums_one[:, :base],
        sums_one[:, base + 2],
        sums_one[:, base + 3],
        sums_two[:, :model_width],
        sums_two[:, model_width + 2],
        sums_two[:, model_width],
        sums_two[:, model_width + 1],
        sums_two[:, model_width + 3 : model_width + 3 + EXPERTS],
        gate_grad_w,
        up_grad_w,
        down_grad,
    )


def solution(mesh):
    in_specs = (
        P(("dp", "seq"), None, None),
        P("dp"),
        P("dp"),
        P("dp", None),
        P("dp"),
        P("dp"),
        P("dp", None),
        P("dp"),
        P("dp"),
        P("dp"),
        P("dp", None),
        P("dp", None, "seq"),
        P("dp", None, "seq"),
        P("dp", "seq", None),
        P(("dp", "seq"), None, None),
        P("dp", None),
        P(("dp", "seq"), None, None),
    )
    out_specs = (
        P(("dp", "seq"), None, None),
        P(("dp", "seq"), None, None),
        P("dp"),
        P("dp"),
        P("dp", None),
        P("dp"),
        P("dp"),
        P("dp", None),
        P("dp"),
        P("dp"),
        P("dp"),
        P("dp", None),
        P("dp", None, "seq"),
        P("dp", None, "seq"),
        P("dp", "seq", None),
    )
    return jax.shard_map(
        per_device, mesh=mesh, in_specs=in_specs, out_specs=out_specs, check_vma=False
    )
```

```python
import math

import jax
import jax.numpy as jnp
from jax import lax
from jax.sharding import PartitionSpec as P


HEAD = 64
EXPERTS = 32
TOP = 2
CAP = 14
CHUNKS = 2
LANES = 128


epsilon = 1e-06
f32 = jnp.float32
bf16 = jnp.bfloat16


def normalize(values, norm_gain, norm_bias):
    average = jnp.mean(values, axis=-1, keepdims=True)
    centred = values - average
    variance = jnp.mean(centred * centred, axis=-1, keepdims=True)
    inverse = lax.rsqrt(variance + epsilon)
    unit_rows = centred * inverse
    scaled = unit_rows * norm_gain + norm_bias
    return (scaled, unit_rows, inverse)


def normalize_back(upstream, unit_rows, inverse, norm_gain):
    scaled = upstream * norm_gain
    mean_term = jnp.mean(scaled, axis=-1, keepdims=True)
    proj_term = jnp.mean(scaled * unit_rows, axis=-1, keepdims=True)
    return inverse * (scaled - mean_term - unit_rows * proj_term)


def gelu_tanh(values):
    return jax.nn.gelu(values, approximate=True)


def dot(a, b, dims):
    return lax.dot_general(a, b, (dims, ((), ())), preferred_element_type=f32)


def partner(tensor, axis, flip):
    size = lax.axis_size(axis)
    return lax.ppermute(tensor, axis, [(i, i ^ flip) for i in range(size)])


def exchange(tensor, axis):
    return lax.all_to_all(tensor, axis, split_axis=0, concat_axis=0, tiled=False)


def spread_all(tensor, axis):
    size = lax.axis_size(axis)
    return exchange(jnp.broadcast_to(tensor[None], (size,) + tensor.shape), axis)


def after(value, *others):
    return lax.optimization_barrier((value,) + others)[0]


def bit_count(axis):
    return (lax.axis_size(axis) - 1).bit_length()


def split_columns(width):
    return (width // 2 // LANES) * LANES


def gather_rows(tensor, halves):
    bits = bit_count("dp")
    if bits == 3:
        first = partner(tensor, "dp", 2)
        second = partner(tensor, "dp", 4)
        if not halves:
            both = partner(first, "dp", 4)
            early = jnp.concatenate([tensor, first, second, both], axis=0)
            return jnp.concatenate([early, partner(early, "dp", 1)], axis=0)
        cut = split_columns(tensor.shape[1])
        pair = [partner(first[:, :cut], "dp", 4), partner(second[:, cut:], "dp", 2)]
        both = jnp.concatenate(pair, axis=1)
        early = jnp.concatenate([tensor, first, second], axis=0)
        early_other = partner(early, "dp", 1)
        both_other = partner(both, "dp", 1)
        return jnp.concatenate([early, both, early_other, both_other], axis=0)
    for bit in list(range(1, bits)) + [0]:
        tensor = jnp.concatenate([tensor, partner(tensor, "dp", 1 << bit)], axis=0)
    return tensor


def place_of(model_width):
    size = lax.axis_size("dp")
    bits = bit_count("dp")
    rows = model_width // size
    feature = jnp.arange(model_width, dtype=jnp.int32)
    relative = (feature // rows) ^ lax.axis_index("dp")
    position = (relative >> 1) + ((relative & 1) << (bits - 1))
    return position * rows + feature % rows


def reduce_rows(wide, narrow):
    size = lax.axis_size("dp")
    bits = bit_count("dp")
    rows = wide.shape[0] // size
    lead = (2,) * (bits - 1)
    totals = []
    for blocks in (wide, narrow):
        width = blocks.shape[1]
        blocks = blocks.reshape(2, size // 2 * rows, width)
        total = blocks[0].astype(f32) + partner(blocks[1], "dp", 1).astype(f32)
        totals.append(total.reshape(lead + (rows, width)))
    cut = split_columns(wide.shape[1] + narrow.shape[1])
    ordinary = list(range(bits - 1, 0, -1))
    parts = []
    for piece, order in (
        (totals[0][..., :cut], ordinary),
        (jnp.concatenate([totals[0][..., cut:], totals[1]], axis=-1), ordinary[::-1]),
    ):
        left = list(ordinary)
        for bit in order:
            axis = left.index(bit)
            keep = lax.index_in_dim(piece, 0, axis, keepdims=False)
            send = lax.index_in_dim(piece, 1, axis, keepdims=False)
            piece = keep + partner(send.astype(bf16), "dp", 1 << bit).astype(f32)
            left.remove(bit)
        parts.append(piece.astype(bf16))
    return jnp.concatenate(parts, axis=1)


def sum_groups(rows):
    groups = lax.axis_size("seq")
    count, width = rows.shape
    shares = exchange(rows.reshape(groups, count // groups, width), "seq")
    total = jnp.sum(shares.astype(f32), axis=0).astype(bf16)
    return spread_all(total, "seq").reshape(count, width).astype(f32)


def program(
    block_input,
    norm1_gain,
    norm1_bias,
    qkv_weight,
    query_bias,
    value_bias,
    out_weight,
    out_bias,
    norm2_gain,
    norm2_bias,
    router_weight,
    gate_weight,
    up_weight,
    down_weight,
    routes,
    key_mask,
    cotangent,
):
    images, tokens, model_width = block_input.shape
    groups = lax.axis_size("seq")
    owners = lax.axis_size("dp")
    pieces = gate_weight.shape[0]
    split_count = owners * pieces // EXPERTS
    head_count = model_width // HEAD
    group_rows = groups * CAP
    me_seq = lax.axis_index("seq")
    me_dp = lax.axis_index("dp")
    inputs = block_input[0]
    upstream = cotangent[0]

    vectors = [norm1_gain, norm1_bias, query_bias, value_bias, out_bias, norm2_gain, norm2_bias]
    small_count = len(vectors) + EXPERTS
    lane_ids = jnp.arange(LANES - EXPERTS, dtype=jnp.int32)
    columns = sum(
        jnp.where(lane_ids == i, vector[:, None], jnp.zeros((), bf16))
        for i, vector in enumerate(vectors)
    )
    qkv_turned = gather_rows(qkv_weight, True)
    gathered = gather_rows(jnp.concatenate([out_weight, router_weight, columns], axis=1), False)
    out_turned = gathered[:, :model_width]
    turn = (
        place_of(model_width)[:, None] == jnp.arange(model_width, dtype=jnp.int32)
    ).astype(bf16)
    small_full = dot(gathered[:, model_width:], turn, ((0,), (1,)))
    gain_one, shift_one, query_full, value_full, obias_full, gain_two, shift_two = [
        small_full[EXPERTS + i] for i in range(len(vectors))
    ]
    router_rows = small_full[:EXPERTS].astype(bf16)

    expert_ids = jnp.arange(EXPERTS, dtype=jnp.int32)
    route_hot = routes[0][..., None] == expert_ids
    per_token = jnp.any(route_hot, axis=1)
    order_ids = jnp.arange(tokens, dtype=jnp.int32)
    before = (order_ids[:, None] > order_ids[None, :]).astype(bf16)
    earlier = dot(before, per_token.astype(bf16), ((1,), (0,)))
    slots = jnp.sum(jnp.where(route_hot, earlier[:, None, :], 0.0), axis=-1)
    labels = jnp.concatenate([routes[0].astype(f32), slots], axis=1)
    labels = jnp.pad(labels, ((0, 0), (0, LANES - 2 * TOP))).astype(bf16)

    def group_tokens(rows):
        others = [partner(rows, "seq", j) for j in range(1, groups)]
        return jnp.concatenate([rows] + others, axis=0)

    cot_group = group_tokens(jnp.concatenate([upstream.astype(bf16), labels], axis=1))
    cot_group = after(cot_group, qkv_turned)
    label_group = cot_group[:, model_width : model_width + 2 * TOP].astype(jnp.int32)
    group_ids = (jnp.arange(groups * tokens, dtype=jnp.int32) // tokens)[:, None] * CAP
    targets = label_group[:, :TOP] * group_rows + group_ids + label_group[:, TOP:]
    slot_ids = jnp.arange(EXPERTS * group_rows, dtype=jnp.int32)
    place = ((targets[:, 0:1] == slot_ids) | (targets[:, 1:2] == slot_ids)).astype(bf16)

    def to_owners(rows):
        width = rows.shape[1]
        filled = dot(place, rows, ((0,), (0,))).astype(bf16)
        filled = filled.reshape(EXPERTS, group_rows, width)
        filled = jnp.repeat(filled, split_count, axis=0) if split_count > 1 else filled
        arrived = exchange(filled.reshape(owners, pieces * group_rows, width), "dp")
        arrived = arrived.reshape(owners, pieces, group_rows, width)
        return jnp.transpose(arrived, (1, 0, 2, 3)).reshape(pieces, owners * group_rows, width)

    def to_sources(rows):
        width = rows.shape[-1]
        rows = rows.reshape(pieces, owners, group_rows, width)
        rows = jnp.transpose(rows, (1, 0, 2, 3)).reshape(owners, pieces * group_rows, width)
        returned = exchange(rows, "dp")
        return returned.reshape(EXPERTS, split_count, group_rows, width)

    def to_tokens(returned):
        width = returned.shape[-1]
        total = None
        for half_index in range(split_count):
            part = dot(
                place, returned[:, half_index].reshape(EXPERTS * group_rows, width), ((1,), (0,))
            )
            total = part if total is None else total + part
        return total.reshape(groups, tokens, width)

    def sum_tokens(parts):
        total = parts[0]
        for j in range(1, groups):
            total = total + partner(parts[j].astype(bf16), "seq", j).astype(f32)
        return total

    cot_rows = to_owners(cot_group[:, :model_width])

    normed_one, unit_one, inverse_one = normalize(inputs, gain_one, shift_one)
    normed_one = normed_one.astype(bf16)
    normed_turned = dot(normed_one, turn, ((1,), (0,))).astype(bf16)
    bias_row = jnp.concatenate([query_full, jnp.zeros((model_width,), f32), value_full])
    projected = (dot(qkv_turned, normed_turned, ((0,), (1,))) + bias_row[:, None]).astype(bf16)
    heads = projected.reshape(3, head_count, HEAD, tokens)
    head_q, head_k, head_v = heads[0], heads[1], heads[2]
    mask_rows = lax.dynamic_slice_in_dim(key_mask, me_seq * images, images, axis=0)
    key_open = mask_rows.astype(f32)[:, None, :]
    scale = 1.0 / math.sqrt(HEAD)
    scores = jnp.einsum("hdq,hdk->hqk", head_q, head_k, preferred_element_type=f32) * scale
    log_total = jnp.log(jnp.sum(jnp.exp(scores) * key_open, axis=-1, keepdims=True))
    probs = jnp.exp(scores - log_total) * key_open
    probs_b = probs.astype(bf16)
    mixed = jnp.einsum("hqk,hdk->hdq", probs_b, head_v, preferred_element_type=f32)
    mixed = mixed.astype(bf16).reshape(model_width, tokens)
    mixed_turned = dot(turn, mixed, ((0,), (0,))).astype(bf16)
    residual_one = inputs + dot(mixed_turned, out_turned, ((0,), (0,))) + obias_full
    normed_two, unit_two, inverse_two = normalize(residual_one, gain_two, shift_two)
    normed_two = normed_two.astype(bf16)

    chunk = model_width // CHUNKS
    spans = [slice(c * chunk, (c + 1) * chunk) for c in range(CHUNKS)]
    hidden_up = jnp.einsum("erd,efd->erf", cot_rows, down_weight, preferred_element_type=f32)
    row_groups = [after(group_tokens(normed_two[:, span]), cot_rows) for span in spans]
    row_chunks = [to_owners(rows) for rows in row_groups]
    gate_pre = up_pre = slot_logits = 0.0
    for rows, span in zip(row_chunks, spans):
        gate_pre = gate_pre + jnp.einsum(
            "erd,edf->erf", rows, gate_weight[:, span], preferred_element_type=f32
        )
        up_pre = up_pre + jnp.einsum(
            "erd,edf->erf", rows, up_weight[:, span], preferred_element_type=f32
        )
        slot_logits = slot_logits + jnp.einsum(
            "erd,nd->ern", rows, router_rows[:, span], preferred_element_type=f32
        )
    slot_exp = jnp.exp(slot_logits)
    piece_ids = me_dp * pieces + jnp.arange(pieces, dtype=jnp.int32)
    mine = (piece_ids // split_count)[:, None, None] == expert_ids
    slot_gate = jnp.sum(jnp.where(mine, slot_exp, 0.0), axis=-1, keepdims=True) / jnp.sum(
        slot_exp, axis=-1, keepdims=True
    )
    activated, gelu_back = jax.vjp(gelu_tanh, gate_pre)
    hidden = (activated * up_pre).astype(bf16)
    slot_score = jnp.sum(hidden.astype(f32) * hidden_up, axis=-1)
    hidden_grad = hidden_up * slot_gate
    gate_pre_grad = gelu_back(hidden_grad * up_pre)[0].astype(bf16)
    up_pre_grad = (hidden_grad * activated).astype(bf16)

    score_high = slot_score.astype(bf16)
    score_low = (slot_score - score_high.astype(f32)).astype(bf16)
    expert_of = (piece_ids // split_count)[:, None, None]
    score_ids = jnp.arange(LANES, dtype=jnp.int32)
    score_columns = jnp.where(expert_of == score_ids, score_high[..., None], 0) + jnp.where(
        expert_of + EXPERTS == score_ids, score_low[..., None], 0
    )
    back_rows = []
    for index, span in enumerate(spans):
        rows_back = jnp.einsum(
            "erf,edf->erd", gate_pre_grad, gate_weight[:, span], preferred_element_type=f32
        ) + jnp.einsum("erf,edf->erd", up_pre_grad, up_weight[:, span], preferred_element_type=f32)
        rows_back = rows_back.astype(bf16)
        if index == 0:
            rows_back = jnp.concatenate([rows_back, score_columns.astype(bf16)], axis=-1)
        back_rows.append(rows_back)
    back_rows, hidden, gate_pre_grad, up_pre_grad = lax.optimization_barrier(
        (back_rows, hidden, gate_pre_grad, up_pre_grad)
    )
    back_chunks = [to_sources(rows) for rows in back_rows]

    out_rows = jnp.einsum("erf,efd->erd", hidden, down_weight, preferred_element_type=f32)
    out_rows = (out_rows * slot_gate).astype(bf16)
    rows_all = jnp.concatenate(row_chunks, axis=-1)
    rows_grad = (cot_rows.astype(f32) * slot_gate).astype(bf16)
    down_grad = jnp.einsum("erf,erd->efd", hidden, rows_grad, preferred_element_type=f32)
    back_sums = [sum_tokens(to_tokens(back_chunks[0]))]
    gate_late = after(gate_pre_grad, back_chunks[0], down_grad)
    up_late = after(up_pre_grad, back_chunks[0], down_grad)
    gate_grad_w = jnp.einsum("erd,erf->edf", rows_all, gate_late, preferred_element_type=f32)
    up_grad_w = jnp.einsum("erd,erf->edf", rows_all, up_late, preferred_element_type=f32)
    back_last, gate_grad_w, up_grad_w = lax.optimization_barrier(
        (back_chunks[1], gate_grad_w, up_grad_w)
    )
    out_rows = after(out_rows, back_last)
    back_sums.append(sum_tokens(to_tokens(back_last)))
    moe_grad = jnp.concatenate([back_sums[0][:, :chunk], back_sums[1]], axis=1)
    spread = (
        back_sums[0][:, chunk : chunk + EXPERTS]
        + back_sums[0][:, chunk + EXPERTS : chunk + 2 * EXPERTS]
    )
    out_returned = to_sources(out_rows)

    logits = dot(normed_two, router_rows, ((1,), (1,)))
    logit_exp = jnp.exp(logits)
    router_probs = logit_exp / jnp.sum(logit_exp, axis=-1, keepdims=True)
    logit_grad = (
        router_probs * (spread - jnp.sum(router_probs * spread, axis=-1, keepdims=True))
    ).astype(bf16)
    router_grad = dot(logit_grad, normed_two, ((0,), (0,)))
    normed_two_grad = moe_grad + dot(logit_grad, router_rows, ((1,), (0,)))
    gain_two_grad = jnp.sum(normed_two_grad * unit_two, axis=0)
    shift_two_grad = jnp.sum(normed_two_grad, axis=0)
    residual_grad = upstream + normalize_back(normed_two_grad, unit_two, inverse_two, gain_two)
    residual_b = residual_grad.astype(bf16)
    out_bias_grad = jnp.sum(residual_grad, axis=0)

    out_blocks = dot(mixed_turned, residual_b, ((1,), (0,))).astype(bf16)
    grad_turned = dot(out_turned, residual_b, ((1,), (1,))).astype(bf16)
    grad_heads = dot(turn, grad_turned, ((1,), (0,))).astype(bf16)
    grad_heads = grad_heads.reshape(head_count, HEAD, tokens)
    probs_grad = jnp.einsum("hdq,hdk->hqk", grad_heads, head_v, preferred_element_type=f32)
    row_term = jnp.sum(probs * probs_grad, axis=-1, keepdims=True)
    score_grad = (probs * (probs_grad - row_term) * scale).astype(bf16)
    value_grad = jnp.einsum(
        "hqk,hdq->hdk", probs_b, grad_heads, preferred_element_type=f32
    ).astype(bf16)
    query_grad = jnp.einsum(
        "hqk,hdk->hdq", score_grad, head_k, preferred_element_type=f32
    ).astype(bf16)
    key_grad = jnp.einsum(
        "hqk,hdq->hdk", score_grad, head_q, preferred_element_type=f32
    ).astype(bf16)
    qkv_grad = jnp.stack([query_grad, key_grad, value_grad]).reshape(3 * model_width, tokens)
    bias_grads = jnp.sum(qkv_grad.astype(f32), axis=1)
    normed_one_back = dot(qkv_grad, qkv_turned, ((0,), (1,)))
    back_high = normed_one_back.astype(bf16)
    back_low = (normed_one_back - back_high.astype(f32)).astype(bf16)
    normed_one_grad = dot(back_high, turn, ((1,), (1,))) + dot(back_low, turn, ((1,), (1,)))
    gain_one_grad = jnp.sum(normed_one_grad * unit_one, axis=0)
    shift_one_grad = jnp.sum(normed_one_grad, axis=0)
    input_grad = residual_grad + normalize_back(normed_one_grad, unit_one, inverse_one, gain_one)

    qkv_blocks = dot(normed_turned, qkv_grad, ((0,), (1,))).astype(bf16)
    out_parts = to_tokens(after(out_returned, qkv_blocks))
    out_tokens = sum_tokens(out_parts)
    small_grads = jnp.concatenate(
        [
            router_grad,
            jnp.stack(
                [
                    gain_one_grad,
                    shift_one_grad,
                    bias_grads[:model_width],
                    bias_grads[2 * model_width :],
                    out_bias_grad,
                    gain_two_grad,
                    shift_two_grad,
                ]
            ),
        ],
        axis=0,
    )
    small_grads = jnp.pad(small_grads, ((0, LANES - small_count), (0, 0))).astype(bf16)
    small_blocks = dot(turn, small_grads, ((0,), (1,))).astype(bf16)
    sums = reduce_rows(qkv_blocks, jnp.concatenate([out_blocks, small_blocks], axis=1))
    sums = sum_groups(after(sums, out_tokens))
    block_output = residual_one + out_tokens

    base = 4 * model_width
    vector_sums = [sums[:, base + EXPERTS + i] for i in range(len(vectors))]
    return (
        block_output[None],
        input_grad[None],
        vector_sums[0],
        vector_sums[1],
        sums[:, : 3 * model_width],
        vector_sums[2],
        vector_sums[3],
        sums[:, 3 * model_width : base],
        vector_sums[4],
        vector_sums[5],
        vector_sums[6],
        sums[:, base : base + EXPERTS],
        gate_grad_w,
        up_grad_w,
        down_grad,
    )


def solution(mesh):
    in_specs = (
        P(("dp", "seq"), None, None),
        P("dp"),
        P("dp"),
        P("dp", None),
        P("dp"),
        P("dp"),
        P("dp", None),
        P("dp"),
        P("dp"),
        P("dp"),
        P("dp", None),
        P("dp", None, "seq"),
        P("dp", None, "seq"),
        P("dp", "seq", None),
        P(("dp", "seq"), None, None),
        P("dp", None),
        P(("dp", "seq"), None, None),
    )
    out_specs = (
        P(("dp", "seq"), None, None),
        P(("dp", "seq"), None, None),
        P("dp"),
        P("dp"),
        P("dp", None),
        P("dp"),
        P("dp"),
        P("dp", None),
        P("dp"),
        P("dp"),
        P("dp"),
        P("dp", None),
        P("dp", None, "seq"),
        P("dp", None, "seq"),
        P("dp", "seq", None),
    )
    return jax.shard_map(
        program, mesh=mesh, in_specs=in_specs, out_specs=out_specs, check_vma=False
    )
```

```python
import functools
import math

import jax
import jax.numpy as jnp
from jax import lax
from jax.experimental import pallas as pl
from jax.experimental.pallas import tpu as pltpu
from jax.sharding import PartitionSpec as P


HEAD = 64
EXPERTS = 32
TOP = 2
CAP = 14
SMALL_CHUNK = 256
LANES = 128


epsilon = 1e-06
f32 = jnp.float32
bf16 = jnp.bfloat16


def normalize(values, norm_gain, norm_bias):
    average = jnp.mean(values, axis=-1, keepdims=True)
    centred = values - average
    variance = jnp.mean(centred * centred, axis=-1, keepdims=True)
    inverse = lax.rsqrt(variance + epsilon)
    unit_rows = centred * inverse
    scaled = unit_rows * norm_gain + norm_bias
    return (scaled, unit_rows, inverse)


def normalize_back(upstream, unit_rows, inverse, norm_gain):
    scaled = upstream * norm_gain
    mean_term = jnp.mean(scaled, axis=-1, keepdims=True)
    proj_term = jnp.mean(scaled * unit_rows, axis=-1, keepdims=True)
    return inverse * (scaled - mean_term - unit_rows * proj_term)


def gelu_tanh(values):
    return jax.nn.gelu(values, approximate=True)


def dot(a, b, dims):
    return lax.dot_general(a, b, (dims, ((), ())), preferred_element_type=f32)


def partner(tensor, axis, flip):
    size = lax.axis_size(axis)
    return lax.ppermute(tensor, axis, [(i, i ^ flip) for i in range(size)])


def exchange(tensor, axis):
    return lax.all_to_all(tensor, axis, split_axis=0, concat_axis=0, tiled=False)


def spread_all(tensor, axis):
    size = lax.axis_size(axis)
    return exchange(jnp.broadcast_to(tensor[None], (size,) + tensor.shape), axis)


def after(value, *others):
    return lax.optimization_barrier((value,) + others)[0]


def bit_count(axis):
    return (lax.axis_size(axis) - 1).bit_length()


def split_columns(width):
    return (width // 2 // LANES) * LANES


def gather_rows(tensor, halves, needed=()):
    bits = bit_count("dp")
    if bits == 3:
        first = partner(tensor, "dp", 2)
        second = partner(tensor, "dp", 4)
        if not halves:
            both = partner(first, "dp", 4)
            early = jnp.concatenate([tensor, first, second, both], axis=0)
            return [early, partner(early, "dp", 1)]
        cut = split_columns(tensor.shape[1])
        pair = [partner(first[:, :cut], "dp", 4), partner(second[:, cut:], "dp", 2)]
        early = after(jnp.concatenate([tensor, first, second], axis=0), *needed)
        both = jnp.concatenate(pair, axis=1)
        early_other = partner(early, "dp", 1)
        both_other = partner(both, "dp", 1)
        return [early, both, early_other, both_other]
    for bit in list(range(1, bits)) + [0]:
        tensor = jnp.concatenate([tensor, partner(tensor, "dp", 1 << bit)], axis=0)
    return [tensor]


def place_of(model_width):
    size = lax.axis_size("dp")
    bits = bit_count("dp")
    rows = model_width // size
    feature = jnp.arange(model_width, dtype=jnp.int32)
    relative = (feature // rows) ^ lax.axis_index("dp")
    position = (relative >> 1) + ((relative & 1) << (bits - 1))
    return position * rows + feature % rows


def reduce_rows(wide, narrow):
    size = lax.axis_size("dp")
    bits = bit_count("dp")
    rows = wide.shape[0] // size
    lead = (2,) * (bits - 1)
    totals = []
    for blocks in (wide, narrow):
        width = blocks.shape[1]
        blocks = blocks.reshape(2, size // 2 * rows, width)
        total = blocks[0].astype(f32) + partner(blocks[1], "dp", 1).astype(f32)
        totals.append(total.reshape(lead + (rows, width)))
    cut = split_columns(wide.shape[1] + narrow.shape[1])
    ordinary = list(range(bits - 1, 0, -1))
    parts = []
    for piece, order in (
        (totals[0][..., :cut], ordinary),
        (jnp.concatenate([totals[0][..., cut:], totals[1]], axis=-1), ordinary[::-1]),
    ):
        left = list(ordinary)
        for bit in order:
            axis = left.index(bit)
            keep = lax.index_in_dim(piece, 0, axis, keepdims=False)
            send = lax.index_in_dim(piece, 1, axis, keepdims=False)
            piece = keep + partner(send.astype(bf16), "dp", 1 << bit).astype(f32)
            left.remove(bit)
        parts.append(piece.astype(bf16))
    return jnp.concatenate(parts, axis=1)


def sum_groups(rows):
    groups = lax.axis_size("seq")
    count, width = rows.shape
    shares = exchange(rows.reshape(groups, count // groups, width), "seq")
    total = jnp.sum(shares.astype(f32), axis=0).astype(bf16)
    return spread_all(total, "seq").reshape(count, width).astype(f32)


def row_tiles(width, tile=256):
    return [(at, min(tile, width - at)) for at in range(0, width, tile)]


def head_mask(which):
    lanes = lax.broadcasted_iota(jnp.int32, (1, 2 * HEAD), 1)
    return (lanes // HEAD == which).astype(f32).astype(bf16)


def assemble(target_ref, piece_refs):
    at = 0
    for piece in piece_refs:
        rows = piece.shape[0]
        target_ref[at : at + rows, :] = piece[...]
        at += rows


def forward_kernel(qkv_count, out_count, cut, *refs):
    qkv_pieces, out_pieces = refs[:qkv_count], refs[qkv_count : qkv_count + out_count]
    (
        input_ref, turn_ref, open_ref,
        turned_ref, proj_ref, probs_ref, mixed_turned_ref, residual_ref, normed_ref, small_ref,
        first_ref, second_ref,
        mixed_ref, qkv_ref, gathered_ref,
    ) = refs[qkv_count + out_count :]
    assemble(qkv_ref, qkv_pieces)
    assemble(gathered_ref, out_pieces)
    width = input_ref.shape[1]
    small_turned = jnp.transpose(gathered_ref[:, width:].astype(f32)).astype(bf16)
    small_ref[...] = dot(small_turned, turn_ref[...], ((1,), (1,)))
    vector = [small_ref[EXPERTS + i : EXPERTS + i + 1, :] for i in range(7)]
    inputs = input_ref[...]
    normed, _, _ = normalize(inputs, vector[0], vector[1])
    turned = dot(normed.astype(bf16), turn_ref[...], ((1,), (0,))).astype(bf16)
    turned_ref[...] = turned
    biases = (vector[2], None, vector[3])
    for section in range(3):
        for at, tile in row_tiles(width):
            columns = slice(section * width + at, section * width + at + tile)
            part = dot(turned, qkv_ref[:, columns], ((1,), (0,)))
            if biases[section] is not None:
                part = part + biases[section][:, at : at + tile]
            proj_ref[:, columns] = part.astype(bf16)
    key_open = open_ref[...]
    scale = 1.0 / math.sqrt(HEAD)
    pair_width = 2 * HEAD

    def pair(index, carry):
        at = pl.multiple_of(index * pair_width, pair_width)
        queries = proj_ref[:, pl.ds(at, pair_width)]
        keys = proj_ref[:, pl.ds(width + at, pair_width)]
        values = proj_ref[:, pl.ds(2 * width + at, pair_width)]
        mixed = None
        for which in range(2):
            mask = head_mask(which)
            scores = dot(queries * mask, keys, ((1,), (1,))) * scale
            weights = jnp.exp(scores) * key_open
            probs = weights * (1.0 / jnp.sum(weights, axis=-1, keepdims=True))
            probs_ref[2 * index + which] = probs
            part = dot(probs.astype(bf16), values * mask, ((1,), (0,)))
            mixed = part if mixed is None else mixed + part
        mixed_ref[:, pl.ds(at, pair_width)] = mixed.astype(bf16)
        return carry

    lax.fori_loop(0, width // pair_width, pair, 0)
    mixed_turned = dot(mixed_ref[...], turn_ref[...], ((1,), (0,))).astype(bf16)
    mixed_turned_ref[...] = mixed_turned
    residual = inputs + dot(mixed_turned, gathered_ref[:, :width], ((1,), (0,))) + vector[4]
    residual_ref[...] = residual
    normed_two, _, _ = normalize(residual, vector[5], vector[6])
    normed_two = normed_two.astype(bf16)
    normed_ref[...] = normed_two
    first_ref[...] = normed_two[:, :cut]
    second_ref[...] = normed_two[:, cut:]


def attention_forward(qkv, gathered, inputs, turn, key_open):
    tokens, width = inputs.shape
    heads = width // HEAD
    shapes = [
        ((tokens, width), bf16),
        ((tokens, 3 * width), bf16),
        ((heads, tokens, tokens), f32),
        ((tokens, width), bf16),
        ((tokens, width), f32),
        ((tokens, width), bf16),
        ((LANES, width), f32),
        ((tokens, SMALL_CHUNK), bf16),
        ((tokens, width - SMALL_CHUNK), bf16),
    ]
    return pl.pallas_call(
        functools.partial(forward_kernel, len(qkv), len(gathered), SMALL_CHUNK),
        out_shape=[jax.ShapeDtypeStruct(shape, kind) for shape, kind in shapes],
        scratch_shapes=[
            pltpu.VMEM((tokens, width), bf16),
            pltpu.VMEM((width, 3 * width), bf16),
            pltpu.VMEM((width, width + LANES), bf16),
        ],
        cost_estimate=pl.CostEstimate(
            flops=2 * tokens * width * (6 * width + 4 * tokens),
            bytes_accessed=16 * width * width,
            transcendentals=heads * tokens * tokens,
        ),
        name="attention_forward",
    )(*qkv, *gathered, inputs, turn, key_open)


def backward_kernel(others, qkv_count, out_count, spread_at, *refs):
    counts = (others + 1, others + 1, qkv_count, out_count)
    lists, at = [], 0
    for count in counts:
        lists.append(refs[at : at + count])
        at += count
    lows, highs, qkv_pieces, out_pieces = lists
    (
        cot_ref, input_ref, residual_ref, normed_ref, turned_ref, proj_ref, probs_ref,
        mixed_turned_ref, small_ref, turn_ref,
        grad_ref, wide_ref, narrow_ref,
        heads_ref, qkv_grad_ref, flip_ref, qkv_ref, gathered_ref,
    ) = refs[at:]
    assemble(qkv_ref, qkv_pieces)
    assemble(gathered_ref, out_pieces)
    _, width = input_ref.shape
    vector = [small_ref[EXPERTS + i : EXPERTS + i + 1, :] for i in range(7)]

    def total(parts):
        result = parts[0][0].astype(f32)
        for part in parts[1:]:
            result = result + part[...].astype(f32)
        return result

    low, high = total(lows), total(highs)
    moe_grad = jnp.concatenate([low[:, :spread_at], high], axis=1)
    spread = low[:, spread_at:]
    _, unit_two, inverse_two = normalize(residual_ref[...], vector[5], vector[6])
    router = small_ref[:LANES, :].astype(bf16)
    logits = dot(normed_ref[...], router, ((1,), (1,)))
    lanes = lax.broadcasted_iota(jnp.int32, (1, LANES), 1)
    weights = jnp.where(lanes < EXPERTS, jnp.exp(jnp.where(lanes < EXPERTS, logits, 0.0)), 0.0)
    router_probs = weights / jnp.sum(weights, axis=-1, keepdims=True)
    logit_grad = (
        router_probs * (spread - jnp.sum(router_probs * spread, axis=-1, keepdims=True))
    ).astype(bf16)
    normed_two_grad = moe_grad + dot(logit_grad, router, ((1,), (0,)))
    residual_grad = cot_ref[...] + normalize_back(
        normed_two_grad, unit_two, inverse_two, vector[5]
    )
    grad_ref[...] = residual_grad
    residual_b = residual_grad.astype(bf16)

    def summed(rows):
        return jnp.sum(rows, axis=0, keepdims=True)

    late = [summed(residual_grad), summed(normed_two_grad * unit_two), summed(normed_two_grad)]
    turn = turn_ref[...]
    heads = dot(residual_b, gathered_ref[:, :width], ((1,), (1,))).astype(bf16)
    heads_ref[...] = dot(heads, turn, ((1,), (1,))).astype(bf16)
    flip_ref[...] = jnp.transpose(mixed_turned_ref[...].astype(f32)).astype(bf16)
    for at, tile in row_tiles(width):
        narrow_ref[:, at : at + tile] = dot(
            flip_ref[...], residual_b[:, at : at + tile], ((1,), (0,))
        ).astype(bf16)
    normed_turned = dot(normed_ref[...], turn, ((1,), (0,)))
    flip_ref[...] = jnp.transpose(normed_turned).astype(bf16)
    router_blocks = dot(flip_ref[...], logit_grad, ((1,), (0,)))

    scale = 1.0 / math.sqrt(HEAD)
    pair_width = 2 * HEAD

    def pair(index, carry):
        at = pl.multiple_of(index * pair_width, pair_width)
        queries = proj_ref[:, pl.ds(at, pair_width)]
        keys = proj_ref[:, pl.ds(width + at, pair_width)]
        values = proj_ref[:, pl.ds(2 * width + at, pair_width)]
        grads = heads_ref[:, pl.ds(at, pair_width)]
        sums = [None, None, None]
        for which in range(2):
            mask = head_mask(which)
            grad = grads * mask
            probs = probs_ref[2 * index + which]
            probs_grad = dot(grad, values, ((1,), (1,)))
            row_term = jnp.sum(probs * probs_grad, axis=-1, keepdims=True)
            score_grad = probs * (probs_grad - row_term) * scale
            parts = (
                dot(score_grad.astype(bf16), keys * mask, ((1,), (0,))),
                dot(jnp.transpose(score_grad).astype(bf16), queries * mask, ((1,), (0,))),
                dot(jnp.transpose(probs).astype(bf16), grad, ((1,), (0,))),
            )
            sums = [p if t is None else t + p for t, p in zip(sums, parts)]
        for section in range(3):
            qkv_grad_ref[:, pl.ds(section * width + at, pair_width)] = sums[section].astype(bf16)
        return carry

    lax.fori_loop(0, width // pair_width, pair, 0)
    flip_ref[...] = jnp.transpose(turned_ref[...].astype(f32)).astype(bf16)
    back = None
    bias_sums = []
    for at, tile in row_tiles(3 * width):
        columns = slice(at, at + tile)
        part_rows = qkv_grad_ref[:, columns]
        wide_ref[:, columns] = dot(flip_ref[...], part_rows, ((1,), (0,))).astype(bf16)
        part = dot(part_rows, qkv_ref[:, columns], ((1,), (1,)))
        back = part if back is None else back + part
        bias_sums.append(summed(part_rows.astype(f32)))
    per_section = len(bias_sums) // 3
    back_high = back.astype(bf16)
    back_low = (back - back_high.astype(f32)).astype(bf16)
    normed_one_grad = dot(back_high, turn, ((1,), (1,))) + dot(back_low, turn, ((1,), (1,)))
    _, unit_one, inverse_one = normalize(input_ref[...], vector[0], vector[1])
    grad_ref[...] = grad_ref[...] + normalize_back(
        normed_one_grad, unit_one, inverse_one, vector[0]
    )
    rows = [
        summed(normed_one_grad * unit_one),
        summed(normed_one_grad),
        jnp.concatenate(bias_sums[:per_section], axis=1),
        jnp.concatenate(bias_sums[2 * per_section :], axis=1),
    ] + late
    table = jnp.concatenate(
        [jnp.zeros((EXPERTS, width), f32)]
        + rows
        + [jnp.zeros((LANES - EXPERTS - len(rows), width), f32)],
        axis=0,
    )
    vector_blocks = jnp.transpose(dot(table.astype(bf16), turn, ((1,), (0,))))
    narrow_ref[:, width:] = (router_blocks + vector_blocks).astype(bf16)


def attention_backward(lows, highs, qkv, gathered, arrays):
    tokens, width = arrays[0].shape
    shapes = [
        ((tokens, width), f32),
        ((width, 3 * width), bf16),
        ((width, width + LANES), bf16),
    ]
    spread_at = lows[0].shape[-1] - LANES
    return pl.pallas_call(
        functools.partial(backward_kernel, len(lows) - 1, len(qkv), len(gathered), spread_at),
        out_shape=[jax.ShapeDtypeStruct(shape, kind) for shape, kind in shapes],
        scratch_shapes=[
            pltpu.VMEM((tokens, width), bf16),
            pltpu.VMEM((tokens, 3 * width), bf16),
            pltpu.VMEM((width, tokens), bf16),
            pltpu.VMEM((width, 3 * width), bf16),
            pltpu.VMEM((width, width + LANES), bf16),
        ],
        cost_estimate=pl.CostEstimate(
            flops=2 * tokens * width * (14 * width + 10 * tokens),
            bytes_accessed=32 * width * width,
            transcendentals=tokens * LANES,
        ),
        name="attention_backward",
    )(*lows, *highs, *qkv, *gathered, *arrays)


def program(
    block_input,
    norm1_gain,
    norm1_bias,
    qkv_weight,
    query_bias,
    value_bias,
    out_weight,
    out_bias,
    norm2_gain,
    norm2_bias,
    router_weight,
    gate_weight,
    up_weight,
    down_weight,
    routes,
    key_mask,
    cotangent,
):
    images, tokens, model_width = block_input.shape
    groups = lax.axis_size("seq")
    owners = lax.axis_size("dp")
    pieces = gate_weight.shape[0]
    split_count = owners * pieces // EXPERTS
    group_rows = groups * CAP
    me_seq = lax.axis_index("seq")
    me_dp = lax.axis_index("dp")
    inputs = block_input[0]
    upstream = cotangent[0]

    vectors = [norm1_gain, norm1_bias, query_bias, value_bias, out_bias, norm2_gain, norm2_bias]
    lane_ids = jnp.arange(LANES - EXPERTS, dtype=jnp.int32)
    columns = sum(
        jnp.where(lane_ids == i, vector[:, None], jnp.zeros((), bf16))
        for i, vector in enumerate(vectors)
    )
    mask_rows = lax.dynamic_slice_in_dim(key_mask, me_seq * images, images, axis=0)
    key_open = mask_rows.astype(f32)
    turn = (
        place_of(model_width)[:, None] == jnp.arange(model_width, dtype=jnp.int32)
    ).astype(bf16)
    qkv_turned = gather_rows(qkv_weight, True, (turn, key_open))
    gathered = gather_rows(jnp.concatenate([out_weight, router_weight, columns], axis=1), False)

    expert_ids = jnp.arange(EXPERTS, dtype=jnp.int32)
    route_hot = routes[0][..., None] == expert_ids
    per_token = jnp.any(route_hot, axis=1)
    order_ids = jnp.arange(tokens, dtype=jnp.int32)
    before = (order_ids[:, None] > order_ids[None, :]).astype(bf16)
    earlier = dot(before, per_token.astype(bf16), ((1,), (0,)))
    slots = jnp.sum(jnp.where(route_hot, earlier[:, None, :], 0.0), axis=-1)
    labels = jnp.concatenate([routes[0].astype(f32), slots], axis=1)
    labels = jnp.pad(labels, ((0, 0), (0, LANES - 2 * TOP))).astype(bf16)

    def group_tokens(rows):
        others = [partner(rows, "seq", j) for j in range(1, groups)]
        return jnp.concatenate([rows] + others, axis=0)

    cot_group = group_tokens(jnp.concatenate([upstream.astype(bf16), labels], axis=1))
    cot_group = after(cot_group, qkv_turned[0])
    label_group = cot_group[:, model_width : model_width + 2 * TOP].astype(jnp.int32)
    group_ids = (jnp.arange(groups * tokens, dtype=jnp.int32) // tokens)[:, None] * CAP
    targets = label_group[:, :TOP] * group_rows + group_ids + label_group[:, TOP:]
    slot_ids = jnp.arange(EXPERTS * group_rows, dtype=jnp.int32)
    place = ((targets[:, 0:1] == slot_ids) | (targets[:, 1:2] == slot_ids)).astype(bf16)

    def to_owners(rows):
        width = rows.shape[1]
        filled = dot(place, rows, ((0,), (0,))).astype(bf16)
        filled = filled.reshape(EXPERTS, group_rows, width)
        filled = jnp.repeat(filled, split_count, axis=0) if split_count > 1 else filled
        return exchange(filled.reshape(owners, pieces * group_rows, width), "dp")

    def by_piece(arrived):
        width = arrived.shape[-1]
        arrived = arrived.reshape(owners, pieces, group_rows, width)
        return jnp.transpose(arrived, (1, 0, 2, 3)).reshape(pieces, owners * group_rows, width)

    def to_sources(rows):
        width = rows.shape[-1]
        rows = rows.reshape(pieces, owners, group_rows, width)
        rows = jnp.transpose(rows, (1, 0, 2, 3)).reshape(owners, pieces * group_rows, width)
        returned = exchange(rows, "dp")
        return returned.reshape(EXPERTS, split_count, group_rows, width)

    def to_tokens(returned):
        width = returned.shape[-1]
        total = None
        for half_index in range(split_count):
            part = dot(
                place, returned[:, half_index].reshape(EXPERTS * group_rows, width), ((1,), (0,))
            )
            total = part if total is None else total + part
        return total.reshape(groups, tokens, width)

    def own_parts(parts):
        parts = parts.astype(bf16)
        return [parts] + [partner(parts[j], "seq", j) for j in range(1, groups)]

    def sum_tokens(parts):
        total = parts[0]
        for j in range(1, groups):
            total = total + partner(parts[j].astype(bf16), "seq", j).astype(f32)
        return total

    cot_arrived = to_owners(cot_group[:, :model_width])
    cot_rows = by_piece(cot_arrived)

    (
        normed_turned, projected, probs, mixed_turned, residual_one, normed_two, small_full,
        *normed_chunks,
    ) = attention_forward(qkv_turned, gathered, inputs, turn, key_open)
    router_rows = small_full[:EXPERTS].astype(bf16)

    spans = [slice(0, SMALL_CHUNK), slice(SMALL_CHUNK, model_width)]
    back_cut = model_width - SMALL_CHUNK
    back_spans = [slice(0, back_cut), slice(back_cut, model_width)]
    hidden_up = jnp.einsum("erd,efd->erf", cot_rows, down_weight, preferred_element_type=f32)
    row_groups = [after(group_tokens(part), cot_arrived) for part in normed_chunks]
    row_chunks = [by_piece(to_owners(rows)) for rows in row_groups]
    gate_pre = up_pre = slot_logits = 0.0
    for rows, span in zip(row_chunks, spans):
        gate_pre = gate_pre + jnp.einsum(
            "erd,edf->erf", rows, gate_weight[:, span], preferred_element_type=f32
        )
        up_pre = up_pre + jnp.einsum(
            "erd,edf->erf", rows, up_weight[:, span], preferred_element_type=f32
        )
        slot_logits = slot_logits + jnp.einsum(
            "erd,nd->ern", rows, router_rows[:, span], preferred_element_type=f32
        )
    slot_exp = jnp.exp(slot_logits)
    piece_ids = me_dp * pieces + jnp.arange(pieces, dtype=jnp.int32)
    mine = (piece_ids // split_count)[:, None, None] == expert_ids
    slot_gate = jnp.sum(jnp.where(mine, slot_exp, 0.0), axis=-1, keepdims=True) / jnp.sum(
        slot_exp, axis=-1, keepdims=True
    )
    activated, gelu_back = jax.vjp(gelu_tanh, gate_pre)
    hidden = (activated * up_pre).astype(bf16)
    slot_score = jnp.sum(hidden.astype(f32) * hidden_up, axis=-1)
    hidden_grad = hidden_up * slot_gate
    gate_pre_grad = gelu_back(hidden_grad * up_pre)[0].astype(bf16)
    up_pre_grad = (hidden_grad * activated).astype(bf16)

    expert_of = (piece_ids // split_count)[:, None, None]
    score_ids = jnp.arange(LANES, dtype=jnp.int32)
    score_columns = jnp.where(expert_of == score_ids, slot_score[..., None], 0.0)
    back_rows = []
    for index, span in enumerate(back_spans):
        rows_back = jnp.einsum(
            "erf,edf->erd", gate_pre_grad, gate_weight[:, span], preferred_element_type=f32
        ) + jnp.einsum("erf,edf->erd", up_pre_grad, up_weight[:, span], preferred_element_type=f32)
        rows_back = rows_back.astype(bf16)
        if index == 0:
            rows_back = jnp.concatenate([rows_back, score_columns.astype(bf16)], axis=-1)
        back_rows.append(rows_back)
    back_rows, hidden, gate_pre_grad, up_pre_grad = lax.optimization_barrier(
        (back_rows, hidden, gate_pre_grad, up_pre_grad)
    )
    back_chunks = [to_sources(rows) for rows in back_rows]

    out_rows = jnp.einsum("erf,efd->erd", hidden, down_weight, preferred_element_type=f32)
    out_rows = (out_rows * slot_gate).astype(bf16)
    rows_all = jnp.concatenate(row_chunks, axis=-1)
    rows_grad = (cot_rows.astype(f32) * slot_gate).astype(bf16)
    down_grad = jnp.einsum("erf,erd->efd", hidden, rows_grad, preferred_element_type=f32)
    gate_grad_w = jnp.einsum("erd,erf->edf", rows_all, gate_pre_grad, preferred_element_type=f32)
    up_grad_w = jnp.einsum("erd,erf->edf", rows_all, up_pre_grad, preferred_element_type=f32)
    back_first, gate_grad_w, up_grad_w, down_grad, out_rows = lax.optimization_barrier(
        (back_chunks[0], gate_grad_w, up_grad_w, down_grad, out_rows)
    )
    lows = own_parts(to_tokens(back_first))
    out_rows = after(out_rows, back_chunks[1])
    last_tokens = to_tokens(back_chunks[1])
    highs = own_parts(last_tokens)
    out_returned = to_sources(out_rows)

    input_grad, qkv_blocks, narrow_blocks = attention_backward(
        lows,
        highs,
        qkv_turned,
        gathered,
        [
            upstream, inputs, residual_one, normed_two, normed_turned, projected, probs,
            mixed_turned, small_full, turn,
        ],
    )
    out_parts = to_tokens(after(out_returned, qkv_blocks))
    out_tokens = sum_tokens(out_parts)
    sums = reduce_rows(qkv_blocks, narrow_blocks)
    sums = sum_groups(sums)
    block_output = residual_one + out_tokens

    base = 4 * model_width
    vector_sums = [sums[:, base + EXPERTS + i] for i in range(len(vectors))]
    return (
        block_output[None],
        input_grad[None],
        vector_sums[0],
        vector_sums[1],
        sums[:, : 3 * model_width],
        vector_sums[2],
        vector_sums[3],
        sums[:, 3 * model_width : base],
        vector_sums[4],
        vector_sums[5],
        vector_sums[6],
        sums[:, base : base + EXPERTS],
        gate_grad_w,
        up_grad_w,
        down_grad,
    )


def solution(mesh):
    in_specs = (
        P(("dp", "seq"), None, None),
        P("dp"),
        P("dp"),
        P("dp", None),
        P("dp"),
        P("dp"),
        P("dp", None),
        P("dp"),
        P("dp"),
        P("dp"),
        P("dp", None),
        P("dp", None, "seq"),
        P("dp", None, "seq"),
        P("dp", "seq", None),
        P(("dp", "seq"), None, None),
        P("dp", None),
        P(("dp", "seq"), None, None),
    )
    out_specs = (
        P(("dp", "seq"), None, None),
        P(("dp", "seq"), None, None),
        P("dp"),
        P("dp"),
        P("dp", None),
        P("dp"),
        P("dp"),
        P("dp", None),
        P("dp"),
        P("dp"),
        P("dp"),
        P("dp", None),
        P("dp", None, "seq"),
        P("dp", None, "seq"),
        P("dp", "seq", None),
    )
    return jax.shard_map(
        program, mesh=mesh, in_specs=in_specs, out_specs=out_specs, check_vma=False
    )
```

```python
import functools
import math

import jax
import jax.numpy as jnp
from jax import lax
from jax.experimental import pallas as pl
from jax.experimental.pallas import tpu as pltpu
from jax.sharding import PartitionSpec as P


HEAD = 64
EXPERTS = 32
TOP = 2
CAP = 14
SMALL_CHUNK = 256
BACK_CHUNK = 384
LANES = 128
TILE = 256


epsilon = 1e-06
f32 = jnp.float32
bf16 = jnp.bfloat16


def normalize(values, norm_gain, norm_bias):
    average = jnp.mean(values, axis=-1, keepdims=True)
    centred = values - average
    variance = jnp.mean(centred * centred, axis=-1, keepdims=True)
    inverse = lax.rsqrt(variance + epsilon)
    unit_rows = centred * inverse
    scaled = unit_rows * norm_gain + norm_bias
    return (scaled, unit_rows, inverse)


def normalize_back(upstream, unit_rows, inverse, norm_gain):
    scaled = upstream * norm_gain
    mean_term = jnp.mean(scaled, axis=-1, keepdims=True)
    proj_term = jnp.mean(scaled * unit_rows, axis=-1, keepdims=True)
    return inverse * (scaled - mean_term - unit_rows * proj_term)


def gelu_tanh(values):
    return jax.nn.gelu(values, approximate=True)


def dot(a, b, dims):
    return lax.dot_general(a, b, (dims, ((), ())), preferred_element_type=f32)


def partner(tensor, axis, flip):
    size = lax.axis_size(axis)
    return lax.ppermute(tensor, axis, [(i, i ^ flip) for i in range(size)])


def exchange(tensor, axis):
    return lax.all_to_all(tensor, axis, split_axis=0, concat_axis=0, tiled=False)


def spread_all(tensor, axis):
    size = lax.axis_size(axis)
    return exchange(jnp.broadcast_to(tensor[None], (size,) + tensor.shape), axis)


def together(*values):
    return lax.optimization_barrier(values)


def bit_count(axis):
    return (lax.axis_size(axis) - 1).bit_length()


def split_columns(width):
    return (width // 2 // LANES) * LANES


def gather_rows(tensor, halves):
    bits = bit_count("dp")
    if bits == 3:
        first = partner(tensor, "dp", 2)
        second = partner(tensor, "dp", 4)
        if not halves:
            both = partner(first, "dp", 4)
            early = jnp.concatenate([tensor, first, second, both], axis=0)
            return [early, partner(early, "dp", 1)]
        cut = split_columns(tensor.shape[1])
        pair = [partner(first[:, :cut], "dp", 4), partner(second[:, cut:], "dp", 2)]
        early = jnp.concatenate([tensor, first, second], axis=0)
        both = jnp.concatenate(pair, axis=1)
        early_other = partner(early, "dp", 1)
        both_other = partner(both, "dp", 1)
        return [early, both, early_other, both_other]
    for bit in list(range(1, bits)) + [0]:
        tensor = jnp.concatenate([tensor, partner(tensor, "dp", 1 << bit)], axis=0)
    return [tensor]


def place_of(model_width):
    size = lax.axis_size("dp")
    bits = bit_count("dp")
    rows = model_width // size
    feature = jnp.arange(model_width, dtype=jnp.int32)
    relative = (feature // rows) ^ lax.axis_index("dp")
    position = (relative >> 1) + ((relative & 1) << (bits - 1))
    return position * rows + feature % rows


def reduce_rows(wide, narrow):
    size = lax.axis_size("dp")
    bits = bit_count("dp")
    rows = 2 * wide[0].shape[0] // size
    lead = (2,) * (bits - 1)
    totals = []
    for keep, send in (wide, narrow):
        total = keep.astype(f32) + partner(send, "dp", 1).astype(f32)
        totals.append(total.reshape(lead + (rows, keep.shape[1])))
    cut = split_columns(wide[0].shape[1] + narrow[0].shape[1])
    ordinary = list(range(bits - 1, 0, -1))
    parts = []
    for piece, order in (
        (totals[0][..., :cut], ordinary),
        (jnp.concatenate([totals[0][..., cut:], totals[1]], axis=-1), ordinary[::-1]),
    ):
        left = list(ordinary)
        for bit in order:
            axis = left.index(bit)
            keep = lax.index_in_dim(piece, 0, axis, keepdims=False)
            send = lax.index_in_dim(piece, 1, axis, keepdims=False)
            piece = keep + partner(send.astype(bf16), "dp", 1 << bit).astype(f32)
            left.remove(bit)
        parts.append(piece.astype(bf16))
    return jnp.concatenate(parts, axis=1)


def sum_groups(rows):
    groups = lax.axis_size("seq")
    count, width = rows.shape
    shares = exchange(rows.reshape(groups, count // groups, width), "seq")
    total = jnp.sum(shares.astype(f32), axis=0).astype(bf16)
    return spread_all(total, "seq").reshape(count, width).astype(f32)


def head_mask(which):
    lanes = lax.broadcasted_iota(jnp.int32, (1, 2 * HEAD), 1)
    return (lanes // HEAD == which).astype(f32).astype(bf16)


def assemble(target_ref, piece_refs, sems):
    copies, at = [], 0
    for index, piece in enumerate(piece_refs):
        rows = piece.shape[0]
        copies.append(
            pltpu.make_async_copy(piece, target_ref.at[at : at + rows, :], sems.at[index])
        )
        at += rows
    for copy in copies:
        copy.start()
    return copies


def wait_all(copies):
    for copy in copies:
        copy.wait()


def forward_kernel(qkv_count, out_count, cut, *refs):
    qkv_pieces, out_pieces = refs[:qkv_count], refs[qkv_count : qkv_count + out_count]
    (
        input_ref, turn_ref, open_ref,
        turned_ref, proj_ref, probs_ref, mixed_turned_ref, residual_ref, normed_ref, small_ref,
        first_ref, second_ref,
        mixed_ref, qkv_ref, gathered_ref, bias_ref, qkv_sems, out_sems,
    ) = refs[qkv_count + out_count :]
    out_copies = assemble(gathered_ref, out_pieces, out_sems)
    qkv_copies = assemble(qkv_ref, qkv_pieces, qkv_sems)
    width = input_ref.shape[1]
    wait_all(out_copies)
    small_turned = jnp.transpose(gathered_ref[:, width:].astype(f32)).astype(bf16)
    small_ref[...] = dot(small_turned, turn_ref[...], ((1,), (1,)))
    vector = [small_ref[EXPERTS + i : EXPERTS + i + 1, :] for i in range(7)]
    inputs = input_ref[...]
    normed, _, _ = normalize(inputs, vector[0], vector[1])
    turned = dot(normed.astype(bf16), turn_ref[...], ((1,), (0,))).astype(bf16)
    turned_ref[...] = turned
    bias_ref[:, :width] = vector[2]
    bias_ref[:, width : 2 * width] = jnp.zeros_like(vector[2])
    bias_ref[:, 2 * width :] = vector[3]

    wait_all(qkv_copies)
    for index in range(3 * width // TILE):
        columns = slice(index * TILE, (index + 1) * TILE)
        part = dot(turned, qkv_ref[:, columns], ((1,), (0,))) + bias_ref[:, columns]
        proj_ref[:, columns] = part.astype(bf16)
    key_open = open_ref[...]
    scale = 1.0 / math.sqrt(HEAD)
    pair_width = 2 * HEAD

    def pair(index, carry):
        at = pl.multiple_of(index * pair_width, pair_width)
        queries = proj_ref[:, pl.ds(at, pair_width)]
        keys = proj_ref[:, pl.ds(width + at, pair_width)]
        values = proj_ref[:, pl.ds(2 * width + at, pair_width)]
        mixed = None
        for which in range(2):
            mask = head_mask(which)
            scores = dot(queries * mask, keys, ((1,), (1,))) * scale
            weights = jnp.exp(scores) * key_open
            probs = weights * (1.0 / jnp.sum(weights, axis=-1, keepdims=True))
            probs_ref[2 * index + which] = probs
            part = dot(probs.astype(bf16), values * mask, ((1,), (0,)))
            mixed = part if mixed is None else mixed + part
        mixed_ref[:, pl.ds(at, pair_width)] = mixed.astype(bf16)
        return carry

    lax.fori_loop(0, width // pair_width, pair, 0)
    mixed_turned = dot(mixed_ref[...], turn_ref[...], ((1,), (0,))).astype(bf16)
    mixed_turned_ref[...] = mixed_turned
    residual = inputs + dot(mixed_turned, gathered_ref[:, :width], ((1,), (0,))) + vector[4]
    residual_ref[...] = residual
    normed_two, _, _ = normalize(residual, vector[5], vector[6])
    normed_two = normed_two.astype(bf16)
    normed_ref[...] = normed_two
    first_ref[...] = normed_two[:, :cut]
    second_ref[...] = normed_two[:, cut:]


def attention_forward(qkv, gathered, inputs, turn, key_open):
    tokens, width = inputs.shape
    heads = width // HEAD
    shapes = [
        ((tokens, width), bf16),
        ((tokens, 3 * width), bf16),
        ((heads, tokens, tokens), f32),
        ((tokens, width), bf16),
        ((tokens, width), f32),
        ((tokens, width), bf16),
        ((LANES, width), f32),
        ((tokens, SMALL_CHUNK), bf16),
        ((tokens, width - SMALL_CHUNK), bf16),
    ]
    return pl.pallas_call(
        functools.partial(forward_kernel, len(qkv), len(gathered), SMALL_CHUNK),
        out_shape=[jax.ShapeDtypeStruct(shape, kind) for shape, kind in shapes],
        scratch_shapes=[
            pltpu.VMEM((tokens, width), bf16),
            pltpu.VMEM((width, 3 * width), bf16),
            pltpu.VMEM((width, width + LANES), bf16),
            pltpu.VMEM((1, 3 * width), f32),
            pltpu.SemaphoreType.DMA((len(qkv),)),
            pltpu.SemaphoreType.DMA((len(gathered),)),
        ],
        in_specs=[pl.BlockSpec(memory_space=pl.ANY)] * (len(qkv) + len(gathered))
        + [pl.BlockSpec(memory_space=pltpu.VMEM)] * 3,
        cost_estimate=pl.CostEstimate(
            flops=2 * tokens * width * (6 * width + 4 * tokens),
            bytes_accessed=16 * width * width,
            transcendentals=heads * tokens * tokens,
        ),
        name="attention_forward",
    )(*qkv, *gathered, inputs, turn, key_open)


def backward_kernel(others, qkv_count, out_count, spread_at, *refs):
    counts = (others + 1, others + 1, qkv_count, out_count)
    lists, at = [], 0
    for count in counts:
        lists.append(refs[at : at + count])
        at += count
    lows, highs, qkv_pieces, out_pieces = lists
    (
        cot_ref, input_ref, residual_ref, normed_ref, turned_ref, proj_ref, probs_ref,
        mixed_turned_ref, small_ref, turn_ref,
        grad_ref, wide_keep, wide_send, narrow_keep, narrow_send,
        heads_ref, qkv_grad_ref, flip_ref, qkv_ref, gathered_ref, bias_ref, probs_scr,
        qkv_sems, out_sems, probs_sem,
    ) = refs[at:]
    out_copies = assemble(gathered_ref, out_pieces, out_sems)
    probs_copy = pltpu.make_async_copy(probs_ref, probs_scr, probs_sem)
    probs_copy.start()
    qkv_copies = assemble(qkv_ref, qkv_pieces, qkv_sems)
    _, width = input_ref.shape
    vector = [small_ref[EXPERTS + i : EXPERTS + i + 1, :] for i in range(7)]

    def total(parts):
        result = parts[0][0].astype(f32)
        for part in parts[1:]:
            result = result + part[...].astype(f32)
        return result

    low, high = total(lows), total(highs)
    moe_grad = jnp.concatenate([low[:, :spread_at], high], axis=1)
    spread = low[:, spread_at:]
    _, unit_two, inverse_two = normalize(residual_ref[...], vector[5], vector[6])
    router = small_ref[:LANES, :].astype(bf16)
    logits = dot(normed_ref[...], router, ((1,), (1,)))
    lanes = lax.broadcasted_iota(jnp.int32, (1, LANES), 1)
    weights = jnp.where(lanes < EXPERTS, jnp.exp(jnp.where(lanes < EXPERTS, logits, 0.0)), 0.0)
    router_probs = weights / jnp.sum(weights, axis=-1, keepdims=True)
    logit_grad = (
        router_probs * (spread - jnp.sum(router_probs * spread, axis=-1, keepdims=True))
    ).astype(bf16)
    normed_two_grad = moe_grad + dot(logit_grad, router, ((1,), (0,)))
    residual_grad = cot_ref[...] + normalize_back(
        normed_two_grad, unit_two, inverse_two, vector[5]
    )
    grad_ref[...] = residual_grad
    residual_b = residual_grad.astype(bf16)

    def summed(rows):
        return jnp.sum(rows, axis=0, keepdims=True)

    late = [summed(residual_grad), summed(normed_two_grad * unit_two), summed(normed_two_grad)]
    turn = turn_ref[...]
    wait_all(out_copies)
    heads = dot(residual_b, gathered_ref[:, :width], ((1,), (1,))).astype(bf16)
    heads_ref[...] = dot(heads, turn, ((1,), (1,))).astype(bf16)
    flip_ref[...] = jnp.transpose(mixed_turned_ref[...].astype(f32)).astype(bf16)
    for index in range(width // TILE):
        columns = slice(index * TILE, (index + 1) * TILE)
        part = dot(flip_ref[...], residual_b[:, columns], ((1,), (0,))).astype(bf16)
        narrow_keep[:, columns] = part[: width // 2]
        narrow_send[:, columns] = part[width // 2 :]
    normed_turned = dot(normed_ref[...], turn, ((1,), (0,)))
    flip_ref[...] = jnp.transpose(normed_turned).astype(bf16)
    router_blocks = dot(flip_ref[...], logit_grad, ((1,), (0,)))

    scale = 1.0 / math.sqrt(HEAD)
    pair_width = 2 * HEAD

    def pair(index, carry):
        at = pl.multiple_of(index * pair_width, pair_width)
        queries = proj_ref[:, pl.ds(at, pair_width)]
        keys = proj_ref[:, pl.ds(width + at, pair_width)]
        values = proj_ref[:, pl.ds(2 * width + at, pair_width)]
        grads = heads_ref[:, pl.ds(at, pair_width)]
        sums = [None, None, None]
        for which in range(2):
            mask = head_mask(which)
            grad = grads * mask
            probs = probs_scr[2 * index + which]
            probs_grad = dot(grad, values, ((1,), (1,)))
            row_term = jnp.sum(probs * probs_grad, axis=-1, keepdims=True)
            score_grad = probs * (probs_grad - row_term) * scale
            parts = (
                dot(score_grad.astype(bf16), keys * mask, ((1,), (0,))),
                dot(jnp.transpose(score_grad).astype(bf16), queries * mask, ((1,), (0,))),
                dot(jnp.transpose(probs).astype(bf16), grad, ((1,), (0,))),
            )
            sums = [p if t is None else t + p for t, p in zip(sums, parts)]
        for section in range(3):
            qkv_grad_ref[:, pl.ds(section * width + at, pair_width)] = sums[section].astype(bf16)
        return carry

    probs_copy.wait()
    lax.fori_loop(0, width // pair_width, pair, 0)
    flip_ref[...] = jnp.transpose(turned_ref[...].astype(f32)).astype(bf16)
    wait_all(qkv_copies)
    back = None
    for index in range(3 * width // TILE):
        columns = slice(index * TILE, (index + 1) * TILE)
        part_rows = qkv_grad_ref[:, columns]
        part = dot(flip_ref[...], part_rows, ((1,), (0,))).astype(bf16)
        wide_keep[:, columns] = part[: width // 2]
        wide_send[:, columns] = part[width // 2 :]
        part = dot(part_rows, qkv_ref[:, columns], ((1,), (1,)))
        back = part if back is None else back + part
        bias_ref[:, columns] = summed(part_rows.astype(f32))
    back_high = back.astype(bf16)
    back_low = (back - back_high.astype(f32)).astype(bf16)
    normed_one_grad = dot(back_high, turn, ((1,), (1,))) + dot(back_low, turn, ((1,), (1,)))
    _, unit_one, inverse_one = normalize(input_ref[...], vector[0], vector[1])
    grad_ref[...] = grad_ref[...] + normalize_back(
        normed_one_grad, unit_one, inverse_one, vector[0]
    )
    rows = [
        summed(normed_one_grad * unit_one),
        summed(normed_one_grad),
        bias_ref[:, :width],
        bias_ref[:, 2 * width :],
    ] + late
    table = jnp.concatenate(
        [jnp.zeros((EXPERTS, width), f32)]
        + rows
        + [jnp.zeros((LANES - EXPERTS - len(rows), width), f32)],
        axis=0,
    )
    vector_blocks = jnp.transpose(dot(table.astype(bf16), turn, ((1,), (0,))))
    small_blocks = (router_blocks + vector_blocks).astype(bf16)
    narrow_keep[:, width:] = small_blocks[: width // 2]
    narrow_send[:, width:] = small_blocks[width // 2 :]


def attention_backward(lows, highs, qkv, gathered, arrays):
    tokens, width = arrays[0].shape
    heads = width // HEAD
    shapes = [
        ((tokens, width), f32),
        ((width // 2, 3 * width), bf16),
        ((width // 2, 3 * width), bf16),
        ((width // 2, width + LANES), bf16),
        ((width // 2, width + LANES), bf16),
    ]
    spread_at = lows[0].shape[-1] - LANES
    return pl.pallas_call(
        functools.partial(backward_kernel, len(lows) - 1, len(qkv), len(gathered), spread_at),
        out_shape=[jax.ShapeDtypeStruct(shape, kind) for shape, kind in shapes],
        scratch_shapes=[
            pltpu.VMEM((tokens, width), bf16),
            pltpu.VMEM((tokens, 3 * width), bf16),
            pltpu.VMEM((width, tokens), bf16),
            pltpu.VMEM((width, 3 * width), bf16),
            pltpu.VMEM((width, width + LANES), bf16),
            pltpu.VMEM((1, 3 * width), f32),
            pltpu.VMEM((heads, tokens, tokens), f32),
            pltpu.SemaphoreType.DMA((len(qkv),)),
            pltpu.SemaphoreType.DMA((len(gathered),)),
            pltpu.SemaphoreType.DMA(()),
        ],
        in_specs=[pl.BlockSpec(memory_space=pltpu.VMEM)] * (2 * len(lows))
        + [pl.BlockSpec(memory_space=pl.ANY)] * (len(qkv) + len(gathered))
        + [
            pl.BlockSpec(memory_space=pl.ANY if index == 6 else pltpu.VMEM)
            for index in range(len(arrays))
        ],
        cost_estimate=pl.CostEstimate(
            flops=2 * tokens * width * (14 * width + 10 * tokens),
            bytes_accessed=32 * width * width,
            transcendentals=tokens * LANES,
        ),
        name="attention_backward",
    )(*lows, *highs, *qkv, *gathered, *arrays)


def program(
    block_input,
    norm1_gain,
    norm1_bias,
    qkv_weight,
    query_bias,
    value_bias,
    out_weight,
    out_bias,
    norm2_gain,
    norm2_bias,
    router_weight,
    gate_weight,
    up_weight,
    down_weight,
    routes,
    key_mask,
    cotangent,
):
    images, tokens, model_width = block_input.shape
    groups = lax.axis_size("seq")
    owners = lax.axis_size("dp")
    pieces = gate_weight.shape[0]
    split_count = owners * pieces // EXPERTS
    group_rows = groups * CAP
    me_seq = lax.axis_index("seq")
    me_dp = lax.axis_index("dp")
    inputs = block_input[0]
    upstream = cotangent[0]

    vectors = [norm1_gain, norm1_bias, query_bias, value_bias, out_bias, norm2_gain, norm2_bias]
    lane_ids = jnp.arange(LANES - EXPERTS, dtype=jnp.int32)
    columns = sum(
        jnp.where(lane_ids == i, vector[:, None], jnp.zeros((), bf16))
        for i, vector in enumerate(vectors)
    )
    mask_rows = lax.dynamic_slice_in_dim(key_mask, me_seq * images, images, axis=0)
    key_open = mask_rows.astype(f32)
    turn = (
        place_of(model_width)[:, None] == jnp.arange(model_width, dtype=jnp.int32)
    ).astype(bf16)
    qkv_turned = gather_rows(qkv_weight, True)
    gathered = gather_rows(jnp.concatenate([out_weight, router_weight, columns], axis=1), False)

    expert_ids = jnp.arange(EXPERTS, dtype=jnp.int32)
    route_hot = routes[0][..., None] == expert_ids
    per_token = jnp.any(route_hot, axis=1)
    order_ids = jnp.arange(tokens, dtype=jnp.int32)
    before = (order_ids[:, None] > order_ids[None, :]).astype(bf16)
    earlier = dot(before, per_token.astype(bf16), ((1,), (0,)))
    slots = jnp.sum(jnp.where(route_hot, earlier[:, None, :], 0.0), axis=-1)
    labels = jnp.concatenate([routes[0].astype(f32), slots], axis=1)
    labels = jnp.pad(labels, ((0, 0), (0, LANES - 2 * TOP))).astype(bf16)

    def group_tokens(rows):
        others = [partner(rows, "seq", j) for j in range(1, groups)]
        return jnp.concatenate([rows] + others, axis=0)

    cot_group = group_tokens(upstream.astype(bf16))
    label_group = group_tokens(labels)
    cot_group, label_group, qkv_turned[-1] = together(cot_group, label_group, qkv_turned[-1])
    labels_across = label_group[:, : 2 * TOP].T.astype(jnp.int32)
    group_ids = jnp.arange(groups * tokens, dtype=jnp.int32) // tokens * CAP
    targets = labels_across[:TOP] * group_rows + group_ids + labels_across[TOP:]
    slot_ids = jnp.arange(EXPERTS * group_rows, dtype=jnp.int32)[:, None]
    place_across = ((targets[0:1] == slot_ids) | (targets[1:2] == slot_ids)).astype(bf16)
    place = place_across.T

    def to_owners(rows, *needed):
        width = rows.shape[1]
        filled = dot(place_across, rows, ((1,), (0,))).astype(bf16)
        filled = filled.reshape(EXPERTS, group_rows, width)
        filled = jnp.repeat(filled, split_count, axis=0) if split_count > 1 else filled
        filled = filled.reshape(owners, pieces * group_rows, width)
        filled, *needed = together(filled, *needed)
        return (exchange(filled, "dp"), *needed)

    def by_piece(arrived):
        width = arrived.shape[-1]
        arrived = arrived.reshape(owners, pieces, group_rows, width)
        return jnp.transpose(arrived, (1, 0, 2, 3)).reshape(pieces, owners * group_rows, width)

    def to_sources(rows):
        width = rows.shape[-1]
        rows = rows.reshape(pieces, owners, group_rows, width)
        rows = jnp.transpose(rows, (1, 0, 2, 3)).reshape(owners, pieces * group_rows, width)
        returned = exchange(rows, "dp")
        return returned.reshape(EXPERTS, split_count, group_rows, width)

    def to_tokens(returned):
        width = returned.shape[-1]
        total = None
        for half_index in range(split_count):
            part = dot(
                place, returned[:, half_index].reshape(EXPERTS * group_rows, width), ((1,), (0,))
            )
            total = part if total is None else total + part
        return total.reshape(groups, tokens, width)

    def own_parts(parts):
        parts = parts.astype(bf16)
        return [parts] + [partner(parts[j], "seq", j) for j in range(1, groups)]

    def sum_tokens(parts):
        total = parts[0]
        for j in range(1, groups):
            total = total + partner(parts[j].astype(bf16), "seq", j).astype(f32)
        return total

    (cot_arrived,) = to_owners(cot_group)

    (
        normed_turned, projected, probs, mixed_turned, residual_one, normed_two, small_full,
        *normed_chunks,
    ) = attention_forward(qkv_turned, gathered, inputs, turn, key_open)
    router_rows = small_full[:EXPERTS].astype(bf16)

    spans = [slice(0, SMALL_CHUNK), slice(SMALL_CHUNK, model_width)]
    back_cut = BACK_CHUNK
    back_spans = [slice(0, back_cut), slice(back_cut, model_width)]
    arrived, cot_arrived = to_owners(group_tokens(normed_chunks[0]), cot_arrived)
    second, arrived = to_owners(group_tokens(normed_chunks[1]), arrived)
    row_chunks = [by_piece(arrived), by_piece(second)]
    cot_rows = by_piece(cot_arrived)
    hidden_up = jnp.einsum("erd,efd->erf", cot_rows, down_weight, preferred_element_type=f32)
    gate_pre = up_pre = slot_logits = 0.0
    for rows, span in zip(row_chunks, spans):
        gate_pre = gate_pre + jnp.einsum(
            "erd,edf->erf", rows, gate_weight[:, span], preferred_element_type=f32
        )
        up_pre = up_pre + jnp.einsum(
            "erd,edf->erf", rows, up_weight[:, span], preferred_element_type=f32
        )
        slot_logits = slot_logits + jnp.einsum(
            "erd,nd->ern", rows, router_rows[:, span], preferred_element_type=f32
        )
    slot_exp = jnp.exp(slot_logits)
    piece_ids = me_dp * pieces + jnp.arange(pieces, dtype=jnp.int32)
    mine = (piece_ids // split_count)[:, None, None] == expert_ids
    slot_gate = jnp.sum(jnp.where(mine, slot_exp, 0.0), axis=-1, keepdims=True) / jnp.sum(
        slot_exp, axis=-1, keepdims=True
    )
    activated, gelu_back = jax.vjp(gelu_tanh, gate_pre)
    hidden = (activated * up_pre).astype(bf16)
    slot_score = jnp.sum(hidden.astype(f32) * hidden_up, axis=-1)
    hidden_grad = hidden_up * slot_gate
    gate_pre_grad = gelu_back(hidden_grad * up_pre)[0].astype(bf16)
    up_pre_grad = (hidden_grad * activated).astype(bf16)

    expert_of = (piece_ids // split_count)[:, None, None]
    score_ids = jnp.arange(LANES, dtype=jnp.int32)
    score_columns = jnp.where(expert_of == score_ids, slot_score[..., None], 0.0)
    back_rows = []
    for index, span in enumerate(back_spans):
        rows_back = jnp.einsum(
            "erf,edf->erd", gate_pre_grad, gate_weight[:, span], preferred_element_type=f32
        ) + jnp.einsum("erf,edf->erd", up_pre_grad, up_weight[:, span], preferred_element_type=f32)
        rows_back = rows_back.astype(bf16)
        if index == 0:
            rows_back = jnp.concatenate([rows_back, score_columns.astype(bf16)], axis=-1)
        back_rows.append(rows_back)
    back_rows, hidden, gate_pre_grad, up_pre_grad = lax.optimization_barrier(
        (back_rows, hidden, gate_pre_grad, up_pre_grad)
    )
    out_rows = jnp.einsum("erf,efd->erd", hidden, down_weight, preferred_element_type=f32)
    out_rows = (out_rows * slot_gate).astype(bf16)
    rows_all = jnp.concatenate(row_chunks, axis=-1)
    rows_grad = (cot_rows.astype(f32) * slot_gate).astype(bf16)
    gate_grad_w = jnp.einsum("erd,erf->edf", rows_all, gate_pre_grad, preferred_element_type=f32)
    up_grad_w = jnp.einsum("erd,erf->edf", rows_all, up_pre_grad, preferred_element_type=f32)
    first_back = to_sources(back_rows[0])
    second_rows, first_back, gate_grad_w, up_grad_w, out_rows = together(
        back_rows[1], first_back, gate_grad_w, up_grad_w, out_rows
    )
    back_chunks = [first_back, to_sources(second_rows)]
    lows = own_parts(to_tokens(back_chunks[0]))
    last_tokens = to_tokens(back_chunks[1])
    last_tokens, out_rows, hidden_late = together(last_tokens, out_rows, hidden)
    highs = own_parts(last_tokens)
    down_grad = jnp.einsum("erf,erd->efd", hidden_late, rows_grad, preferred_element_type=f32)
    out_returned = to_sources(out_rows)

    upstream, down_grad = together(upstream, down_grad)
    input_grad, *grad_blocks = attention_backward(
        lows,
        highs,
        qkv_turned,
        gathered,
        [
            upstream, inputs, residual_one, normed_two,
            normed_turned, projected, probs, mixed_turned, small_full, turn,
        ],
    )
    out_parts = to_tokens(out_returned)
    out_tokens = sum_tokens(out_parts)
    sums = reduce_rows(grad_blocks[:2], grad_blocks[2:])
    sums = sum_groups(sums)
    block_output = residual_one + out_tokens

    base = 4 * model_width
    vector_sums = [sums[:, base + EXPERTS + i] for i in range(len(vectors))]
    return (
        block_output[None],
        input_grad[None],
        vector_sums[0],
        vector_sums[1],
        sums[:, : 3 * model_width],
        vector_sums[2],
        vector_sums[3],
        sums[:, 3 * model_width : base],
        vector_sums[4],
        vector_sums[5],
        vector_sums[6],
        sums[:, base : base + EXPERTS],
        gate_grad_w,
        up_grad_w,
        down_grad,
    )


def solution(mesh):
    in_specs = (
        P(("dp", "seq"), None, None),
        P("dp"),
        P("dp"),
        P("dp", None),
        P("dp"),
        P("dp"),
        P("dp", None),
        P("dp"),
        P("dp"),
        P("dp"),
        P("dp", None),
        P("dp", None, "seq"),
        P("dp", None, "seq"),
        P("dp", "seq", None),
        P(("dp", "seq"), None, None),
        P("dp", None),
        P(("dp", "seq"), None, None),
    )
    out_specs = (
        P(("dp", "seq"), None, None),
        P(("dp", "seq"), None, None),
        P("dp"),
        P("dp"),
        P("dp", None),
        P("dp"),
        P("dp"),
        P("dp", None),
        P("dp"),
        P("dp"),
        P("dp"),
        P("dp", None),
        P("dp", None, "seq"),
        P("dp", None, "seq"),
        P("dp", "seq", None),
    )
    return jax.shard_map(
        program, mesh=mesh, in_specs=in_specs, out_specs=out_specs, check_vma=False
    )
```

```python
import functools
import math

import jax
import jax.numpy as jnp
from jax import lax
from jax.experimental import pallas as pl
from jax.experimental.pallas import tpu as pltpu
from jax.sharding import PartitionSpec as P


HEAD = 64
EXPERTS = 32
TOP = 2
CAP = 14
SMALL_CHUNK = 256
BACK_CHUNK = 384
LANES = 128
TILE = 256


epsilon = 1e-06
DP, SEQ = "dp", "seq"
f32 = jnp.float32
bf16 = jnp.bfloat16


def normalize(values, norm_gain, norm_bias):
    average = jnp.mean(values, axis=-1, keepdims=True)
    centred = values - average
    variance = jnp.mean(centred * centred, axis=-1, keepdims=True)
    inverse = lax.rsqrt(variance + epsilon)
    unit_rows = centred * inverse
    scaled = unit_rows * norm_gain + norm_bias
    return (scaled, unit_rows, inverse)


def normalize_back(upstream, unit_rows, inverse, norm_gain):
    scaled = upstream * norm_gain
    mean_term = jnp.mean(scaled, axis=-1, keepdims=True)
    proj_term = jnp.mean(scaled * unit_rows, axis=-1, keepdims=True)
    return inverse * (scaled - mean_term - unit_rows * proj_term)


def gelu_tanh(values):
    return jax.nn.gelu(values, approximate=True)


def dot(a, b, dims):
    return lax.dot_general(a, b, (dims, ((), ())), preferred_element_type=f32)


def partner(tensor, axis, flip):
    size = lax.axis_size(axis)
    return lax.ppermute(tensor, axis, [(i, i ^ flip) for i in range(size)])


def exchange(tensor, axis):
    return lax.all_to_all(tensor, axis, split_axis=0, concat_axis=0, tiled=False)


def spread_all(tensor, axis):
    size = lax.axis_size(axis)
    return exchange(jnp.broadcast_to(tensor[None], (size,) + tensor.shape), axis)


def together(*values):
    return lax.optimization_barrier(values)


def bit_count(axis):
    return (lax.axis_size(axis) - 1).bit_length()


def split_columns(width):
    return (width // 2 // LANES) * LANES


def gather_rows(tensor, halves):
    bits = bit_count(DP)
    if bits == 3:
        first = partner(tensor, DP, 2)
        second = partner(tensor, DP, 4)
        if not halves:
            both = partner(first, DP, 4)
            early = jnp.concatenate([tensor, first, second, both], axis=0)
            return [early, partner(early, DP, 1)]
        cut = split_columns(tensor.shape[1])
        pair = [partner(first[:, :cut], DP, 4), partner(second[:, cut:], DP, 2)]
        early = jnp.concatenate([tensor, first, second], axis=0)
        both = jnp.concatenate(pair, axis=1)
        early_other = partner(early, DP, 1)
        both_other = partner(both, DP, 1)
        return [early, both, early_other, both_other]
    for bit in list(range(1, bits)) + [0]:
        tensor = jnp.concatenate([tensor, partner(tensor, DP, 1 << bit)], axis=0)
    return [tensor]


def place_of(model_width):
    size = lax.axis_size(DP)
    bits = bit_count(DP)
    rows = model_width // size
    feature = jnp.arange(model_width, dtype=jnp.int32)
    relative = (feature // rows) ^ lax.axis_index(DP)
    position = (relative >> 1) + ((relative & 1) << (bits - 1))
    return position * rows + feature % rows


def reduce_rows(wide, narrow):
    size = lax.axis_size(DP)
    bits = bit_count(DP)
    rows = 2 * wide[0].shape[0] // size
    lead = (2,) * (bits - 1)
    totals = []
    for keep, send in (wide, narrow):
        total = keep.astype(f32) + partner(send, DP, 1).astype(f32)
        totals.append(total.reshape(lead + (rows, keep.shape[1])))
    cut = split_columns(wide[0].shape[1] + narrow[0].shape[1])
    ordinary = list(range(bits - 1, 0, -1))
    parts = []
    for piece, order in (
        (totals[0][..., :cut], ordinary),
        (jnp.concatenate([totals[0][..., cut:], totals[1]], axis=-1), ordinary[::-1]),
    ):
        left = list(ordinary)
        for bit in order:
            axis = left.index(bit)
            keep = lax.index_in_dim(piece, 0, axis, keepdims=False)
            send = lax.index_in_dim(piece, 1, axis, keepdims=False)
            piece = keep + partner(send.astype(bf16), DP, 1 << bit).astype(f32)
            left.remove(bit)
        parts.append(piece.astype(bf16))
    return jnp.concatenate(parts, axis=1)


def sum_groups(rows):
    groups = lax.axis_size(SEQ)
    count, width = rows.shape
    shares = exchange(rows.reshape(groups, count // groups, width), SEQ)
    total = jnp.sum(shares.astype(f32), axis=0).astype(bf16)
    return spread_all(total, SEQ).reshape(count, width).astype(f32)


def head_mask(which):
    lanes = lax.broadcasted_iota(jnp.int32, (1, 2 * HEAD), 1)
    return (lanes // HEAD == which).astype(f32).astype(bf16)


def assemble(target_ref, piece_refs, sems):
    copies, at = [], 0
    for index, piece in enumerate(piece_refs):
        rows = piece.shape[0]
        copies.append(
            pltpu.make_async_copy(piece, target_ref.at[at : at + rows, :], sems.at[index])
        )
        at += rows
    for copy in copies:
        copy.start()
    return copies


def wait_all(copies):
    for copy in copies:
        copy.wait()


def forward_kernel(qkv_count, out_count, cut, *refs):
    qkv_pieces, out_pieces = refs[:qkv_count], refs[qkv_count : qkv_count + out_count]
    (
        input_ref, turn_ref, open_ref,
        turned_ref, proj_ref, probs_ref, mixed_turned_ref, residual_ref, normed_ref, small_ref,
        first_ref, second_ref,
        mixed_ref, qkv_ref, gathered_ref, bias_ref, qkv_sems, out_sems,
    ) = refs[qkv_count + out_count :]
    out_copies = assemble(gathered_ref, out_pieces, out_sems)
    qkv_copies = assemble(qkv_ref, qkv_pieces, qkv_sems)
    width = input_ref.shape[1]
    wait_all(out_copies)
    small_turned = jnp.transpose(gathered_ref[:, width:].astype(f32)).astype(bf16)
    small_ref[...] = dot(small_turned, turn_ref[...], ((1,), (1,)))
    vector = [small_ref[EXPERTS + i : EXPERTS + i + 1, :] for i in range(7)]
    inputs = input_ref[...]
    normed, _, _ = normalize(inputs, vector[0], vector[1])
    turned = dot(normed.astype(bf16), turn_ref[...], ((1,), (0,))).astype(bf16)
    turned_ref[...] = turned
    bias_ref[:, :width] = vector[2]
    bias_ref[:, width : 2 * width] = jnp.zeros_like(vector[2])
    bias_ref[:, 2 * width :] = vector[3]

    wait_all(qkv_copies)
    for index in range(3 * width // TILE):
        columns = slice(index * TILE, (index + 1) * TILE)
        part = dot(turned, qkv_ref[:, columns], ((1,), (0,))) + bias_ref[:, columns]
        proj_ref[:, columns] = part.astype(bf16)
    key_open = open_ref[...]
    scale = 1.0 / math.sqrt(HEAD)
    pair_width = 2 * HEAD

    def pair(index, carry):
        at = pl.multiple_of(index * pair_width, pair_width)
        queries = proj_ref[:, pl.ds(at, pair_width)]
        keys = proj_ref[:, pl.ds(width + at, pair_width)]
        values = proj_ref[:, pl.ds(2 * width + at, pair_width)]
        mixed = None
        for which in range(2):
            mask = head_mask(which)
            scores = dot(queries * mask, keys, ((1,), (1,))) * scale
            weights = jnp.exp(scores) * key_open
            probs = weights * (1.0 / jnp.sum(weights, axis=-1, keepdims=True))
            probs_ref[2 * index + which] = probs
            part = dot(probs.astype(bf16), values * mask, ((1,), (0,)))
            mixed = part if mixed is None else mixed + part
        mixed_ref[:, pl.ds(at, pair_width)] = mixed.astype(bf16)
        return carry

    lax.fori_loop(0, width // pair_width, pair, 0)
    mixed_turned = dot(mixed_ref[...], turn_ref[...], ((1,), (0,))).astype(bf16)
    mixed_turned_ref[...] = mixed_turned
    residual = inputs + dot(mixed_turned, gathered_ref[:, :width], ((1,), (0,))) + vector[4]
    residual_ref[...] = residual
    normed_two, _, _ = normalize(residual, vector[5], vector[6])
    normed_two = normed_two.astype(bf16)
    normed_ref[...] = normed_two
    first_ref[...] = normed_two[:, :cut]
    second_ref[...] = normed_two[:, cut:]


def attention_forward(qkv, gathered, inputs, turn, key_open):
    tokens, width = inputs.shape
    heads = width // HEAD
    shapes = [
        ((tokens, width), bf16),
        ((tokens, 3 * width), bf16),
        ((heads, tokens, tokens), f32),
        ((tokens, width), bf16),
        ((tokens, width), f32),
        ((tokens, width), bf16),
        ((LANES, width), f32),
        ((tokens, SMALL_CHUNK), bf16),
        ((tokens, width - SMALL_CHUNK), bf16),
    ]
    return pl.pallas_call(
        functools.partial(forward_kernel, len(qkv), len(gathered), SMALL_CHUNK),
        out_shape=[jax.ShapeDtypeStruct(shape, kind) for shape, kind in shapes],
        scratch_shapes=[
            pltpu.VMEM((tokens, width), bf16),
            pltpu.VMEM((width, 3 * width), bf16),
            pltpu.VMEM((width, width + LANES), bf16),
            pltpu.VMEM((1, 3 * width), f32),
            pltpu.SemaphoreType.DMA((len(qkv),)),
            pltpu.SemaphoreType.DMA((len(gathered),)),
        ],
        in_specs=[pl.BlockSpec(memory_space=pl.ANY)] * (len(qkv) + len(gathered))
        + [pl.BlockSpec(memory_space=pltpu.VMEM)] * 3,
        cost_estimate=pl.CostEstimate(
            flops=2 * tokens * width * (6 * width + 4 * tokens),
            bytes_accessed=16 * width * width,
            transcendentals=heads * tokens * tokens,
        ),
        name="forward",
    )(*qkv, *gathered, inputs, turn, key_open)


def backward_kernel(others, qkv_count, out_count, spread_at, *refs):
    counts = (others + 1, others + 1, qkv_count, out_count)
    lists, at = [], 0
    for count in counts:
        lists.append(refs[at : at + count])
        at += count
    lows, highs, qkv_pieces, out_pieces = lists
    (
        cot_ref, input_ref, residual_ref, normed_ref, turned_ref, proj_ref, probs_ref,
        mixed_turned_ref, small_ref, turn_ref,
        grad_ref, wide_keep, wide_send, narrow_keep, narrow_send,
        heads_ref, qkv_grad_ref, flip_ref, qkv_ref, gathered_ref, bias_ref, probs_scr,
        qkv_sems, out_sems, probs_sem,
    ) = refs[at:]
    out_copies = assemble(gathered_ref, out_pieces, out_sems)
    probs_copy = pltpu.make_async_copy(probs_ref, probs_scr, probs_sem)
    probs_copy.start()
    qkv_copies = assemble(qkv_ref, qkv_pieces, qkv_sems)
    _, width = input_ref.shape
    vector = [small_ref[EXPERTS + i : EXPERTS + i + 1, :] for i in range(7)]

    def total(parts):
        result = parts[0][0].astype(f32)
        for part in parts[1:]:
            result = result + part[...].astype(f32)
        return result

    low, high = total(lows), total(highs)
    moe_grad = jnp.concatenate([low[:, :spread_at], high], axis=1)
    spread = low[:, spread_at:]
    _, unit_two, inverse_two = normalize(residual_ref[...], vector[5], vector[6])
    router = small_ref[:LANES, :].astype(bf16)
    logits = dot(normed_ref[...], router, ((1,), (1,)))
    lanes = lax.broadcasted_iota(jnp.int32, (1, LANES), 1)
    weights = jnp.where(lanes < EXPERTS, jnp.exp(jnp.where(lanes < EXPERTS, logits, 0.0)), 0.0)
    router_probs = weights / jnp.sum(weights, axis=-1, keepdims=True)
    logit_grad = (
        router_probs * (spread - jnp.sum(router_probs * spread, axis=-1, keepdims=True))
    ).astype(bf16)
    normed_two_grad = moe_grad + dot(logit_grad, router, ((1,), (0,)))
    residual_grad = cot_ref[...] + normalize_back(
        normed_two_grad, unit_two, inverse_two, vector[5]
    )
    grad_ref[...] = residual_grad
    residual_b = residual_grad.astype(bf16)

    def summed(rows):
        return jnp.sum(rows, axis=0, keepdims=True)

    late = [summed(residual_grad), summed(normed_two_grad * unit_two), summed(normed_two_grad)]
    turn = turn_ref[...]
    wait_all(out_copies)
    heads = dot(residual_b, gathered_ref[:, :width], ((1,), (1,))).astype(bf16)
    heads_ref[...] = dot(heads, turn, ((1,), (1,))).astype(bf16)
    flip_ref[...] = jnp.transpose(mixed_turned_ref[...].astype(f32)).astype(bf16)
    for index in range(width // TILE):
        columns = slice(index * TILE, (index + 1) * TILE)
        part = dot(flip_ref[...], residual_b[:, columns], ((1,), (0,))).astype(bf16)
        narrow_keep[:, columns] = part[: width // 2]
        narrow_send[:, columns] = part[width // 2 :]
    normed_turned = dot(normed_ref[...], turn, ((1,), (0,)))
    flip_ref[...] = jnp.transpose(normed_turned).astype(bf16)
    router_blocks = dot(flip_ref[...], logit_grad, ((1,), (0,)))

    scale = 1.0 / math.sqrt(HEAD)
    pair_width = 2 * HEAD

    def pair(index, carry):
        at = pl.multiple_of(index * pair_width, pair_width)
        queries = proj_ref[:, pl.ds(at, pair_width)]
        keys = proj_ref[:, pl.ds(width + at, pair_width)]
        values = proj_ref[:, pl.ds(2 * width + at, pair_width)]
        grads = heads_ref[:, pl.ds(at, pair_width)]
        sums = [None, None, None]
        for which in range(2):
            mask = head_mask(which)
            grad = grads * mask
            probs = probs_scr[2 * index + which]
            probs_grad = dot(grad, values, ((1,), (1,)))
            row_term = jnp.sum(probs * probs_grad, axis=-1, keepdims=True)
            score_grad = probs * (probs_grad - row_term) * scale
            parts = (
                dot(score_grad.astype(bf16), keys * mask, ((1,), (0,))),
                dot(jnp.transpose(score_grad).astype(bf16), queries * mask, ((1,), (0,))),
                dot(jnp.transpose(probs).astype(bf16), grad, ((1,), (0,))),
            )
            sums = [p if t is None else t + p for t, p in zip(sums, parts)]
        for section in range(3):
            qkv_grad_ref[:, pl.ds(section * width + at, pair_width)] = sums[section].astype(bf16)
        return carry

    probs_copy.wait()
    lax.fori_loop(0, width // pair_width, pair, 0)
    flip_ref[...] = jnp.transpose(turned_ref[...].astype(f32)).astype(bf16)
    wait_all(qkv_copies)
    back = None
    for index in range(3 * width // TILE):
        columns = slice(index * TILE, (index + 1) * TILE)
        part_rows = qkv_grad_ref[:, columns]
        part = dot(flip_ref[...], part_rows, ((1,), (0,))).astype(bf16)
        wide_keep[:, columns] = part[: width // 2]
        wide_send[:, columns] = part[width // 2 :]
        part = dot(part_rows, qkv_ref[:, columns], ((1,), (1,)))
        back = part if back is None else back + part
        bias_ref[:, columns] = summed(part_rows.astype(f32))
    back_high = back.astype(bf16)
    back_low = (back - back_high.astype(f32)).astype(bf16)
    normed_one_grad = dot(back_high, turn, ((1,), (1,))) + dot(back_low, turn, ((1,), (1,)))
    _, unit_one, inverse_one = normalize(input_ref[...], vector[0], vector[1])
    grad_ref[...] = grad_ref[...] + normalize_back(
        normed_one_grad, unit_one, inverse_one, vector[0]
    )
    rows = [
        summed(normed_one_grad * unit_one),
        summed(normed_one_grad),
        bias_ref[:, :width],
        bias_ref[:, 2 * width :],
    ] + late
    table = jnp.concatenate(
        [jnp.zeros((EXPERTS, width), f32)]
        + rows
        + [jnp.zeros((LANES - EXPERTS - len(rows), width), f32)],
        axis=0,
    )
    vector_blocks = jnp.transpose(dot(table.astype(bf16), turn, ((1,), (0,))))
    small_blocks = (router_blocks + vector_blocks).astype(bf16)
    narrow_keep[:, width:] = small_blocks[: width // 2]
    narrow_send[:, width:] = small_blocks[width // 2 :]


def attention_backward(lows, highs, qkv, gathered, arrays):
    tokens, width = arrays[0].shape
    heads = width // HEAD
    shapes = [
        ((tokens, width), f32),
        ((width // 2, 3 * width), bf16),
        ((width // 2, 3 * width), bf16),
        ((width // 2, width + LANES), bf16),
        ((width // 2, width + LANES), bf16),
    ]
    spread_at = lows[0].shape[-1] - LANES
    return pl.pallas_call(
        functools.partial(backward_kernel, len(lows) - 1, len(qkv), len(gathered), spread_at),
        out_shape=[jax.ShapeDtypeStruct(shape, kind) for shape, kind in shapes],
        scratch_shapes=[
            pltpu.VMEM((tokens, width), bf16),
            pltpu.VMEM((tokens, 3 * width), bf16),
            pltpu.VMEM((width, tokens), bf16),
            pltpu.VMEM((width, 3 * width), bf16),
            pltpu.VMEM((width, width + LANES), bf16),
            pltpu.VMEM((1, 3 * width), f32),
            pltpu.VMEM((heads, tokens, tokens), f32),
            pltpu.SemaphoreType.DMA((len(qkv),)),
            pltpu.SemaphoreType.DMA((len(gathered),)),
            pltpu.SemaphoreType.DMA(()),
        ],
        in_specs=[pl.BlockSpec(memory_space=pltpu.VMEM)] * (2 * len(lows))
        + [pl.BlockSpec(memory_space=pl.ANY)] * (len(qkv) + len(gathered))
        + [
            pl.BlockSpec(memory_space=pl.ANY if index == 6 else pltpu.VMEM)
            for index in range(len(arrays))
        ],
        cost_estimate=pl.CostEstimate(
            flops=2 * tokens * width * (14 * width + 10 * tokens),
            bytes_accessed=32 * width * width,
            transcendentals=tokens * LANES,
        ),
        name="backward",
    )(*lows, *highs, *qkv, *gathered, *arrays)


def program(
    block_input,
    norm1_gain,
    norm1_bias,
    qkv_weight,
    query_bias,
    value_bias,
    out_weight,
    out_bias,
    norm2_gain,
    norm2_bias,
    router_weight,
    gate_weight,
    up_weight,
    down_weight,
    routes,
    key_mask,
    cotangent,
):
    images, tokens, model_width = block_input.shape
    groups = lax.axis_size(SEQ)
    owners = lax.axis_size(DP)
    pieces = gate_weight.shape[0]
    split_count = owners * pieces // EXPERTS
    group_rows = groups * CAP
    me_seq = lax.axis_index(SEQ)
    me_dp = lax.axis_index(DP)
    inputs = block_input[0]
    upstream = cotangent[0]

    vectors = [norm1_gain, norm1_bias, query_bias, value_bias, out_bias, norm2_gain, norm2_bias]
    lane_ids = jnp.arange(LANES - EXPERTS, dtype=jnp.int32)
    columns = sum(
        jnp.where(lane_ids == i, vector[:, None], jnp.zeros((), bf16))
        for i, vector in enumerate(vectors)
    )
    mask_rows = lax.dynamic_slice_in_dim(key_mask, me_seq * images, images, axis=0)
    key_open = mask_rows.astype(f32)
    turn = (
        place_of(model_width)[:, None] == jnp.arange(model_width, dtype=jnp.int32)
    ).astype(bf16)
    qkv_turned = gather_rows(qkv_weight, True)
    gathered = gather_rows(jnp.concatenate([out_weight, router_weight, columns], axis=1), False)

    expert_ids = jnp.arange(EXPERTS, dtype=jnp.int32)
    route_hot = routes[0][..., None] == expert_ids
    per_token = jnp.any(route_hot, axis=1)
    order_ids = jnp.arange(tokens, dtype=jnp.int32)
    before = (order_ids[:, None] > order_ids[None, :]).astype(bf16)
    earlier = dot(before, per_token.astype(bf16), ((1,), (0,)))
    slots = jnp.sum(jnp.where(route_hot, earlier[:, None, :], 0.0), axis=-1)
    labels = jnp.concatenate([routes[0].astype(f32), slots], axis=1)
    labels = jnp.pad(labels, ((0, 0), (0, LANES - 2 * TOP))).astype(bf16)

    def group_tokens(rows):
        others = [partner(rows, SEQ, j) for j in range(1, groups)]
        return jnp.concatenate([rows] + others, axis=0)

    cot_group = group_tokens(upstream.astype(bf16))
    label_group = group_tokens(labels)
    cot_group, label_group, qkv_turned[-1] = together(cot_group, label_group, qkv_turned[-1])
    labels_across = label_group[:, : 2 * TOP].T.astype(jnp.int32)
    group_ids = jnp.arange(groups * tokens, dtype=jnp.int32) // tokens * CAP
    targets = labels_across[:TOP] * group_rows + group_ids + labels_across[TOP:]
    slot_ids = jnp.arange(EXPERTS * group_rows, dtype=jnp.int32)[:, None]
    place_across = ((targets[0:1] == slot_ids) | (targets[1:2] == slot_ids)).astype(bf16)
    place = place_across.T

    def to_owners(rows, *needed):
        width = rows.shape[1]
        filled = dot(place_across, rows, ((1,), (0,))).astype(bf16)
        filled = filled.reshape(EXPERTS, group_rows, width)
        filled = jnp.repeat(filled, split_count, axis=0) if split_count > 1 else filled
        filled = filled.reshape(owners, pieces * group_rows, width)
        filled, *needed = together(filled, *needed)
        return (exchange(filled, DP), *needed)

    def by_piece(arrived):
        width = arrived.shape[-1]
        arrived = arrived.reshape(owners, pieces, group_rows, width)
        return jnp.transpose(arrived, (1, 0, 2, 3)).reshape(pieces, owners * group_rows, width)

    def by_owner(rows):
        width = rows.shape[-1]
        rows = rows.reshape(pieces, owners, group_rows, width)
        return jnp.transpose(rows, (1, 0, 2, 3)).reshape(owners, pieces * group_rows, width)

    def to_sources(rows):
        returned = exchange(rows, DP)
        return returned.reshape(EXPERTS, split_count, group_rows, rows.shape[-1])

    def to_tokens(returned):
        width = returned.shape[-1]
        total = None
        for half_index in range(split_count):
            part = dot(
                place, returned[:, half_index].reshape(EXPERTS * group_rows, width), ((1,), (0,))
            )
            total = part if total is None else total + part
        return total.reshape(groups, tokens, width)

    def own_parts(parts):
        parts = parts.astype(bf16)
        return [parts] + [partner(parts[j], SEQ, j) for j in range(1, groups)]

    def sum_tokens(parts):
        total = parts[0]
        for j in range(1, groups):
            total = total + partner(parts[j].astype(bf16), SEQ, j).astype(f32)
        return total

    (cot_arrived,) = to_owners(cot_group)

    (
        normed_turned, projected, probs, mixed_turned, residual_one, normed_two, small_full,
        *normed_chunks,
    ) = attention_forward(qkv_turned, gathered, inputs, turn, key_open)
    router_rows = small_full[:EXPERTS].astype(bf16)

    spans = [slice(0, SMALL_CHUNK), slice(SMALL_CHUNK, model_width)]
    back_cut = BACK_CHUNK
    back_spans = [slice(0, back_cut), slice(back_cut, model_width)]
    arrived, cot_arrived = to_owners(group_tokens(normed_chunks[0]), cot_arrived)
    second, arrived = to_owners(group_tokens(normed_chunks[1]), arrived)
    row_chunks = [by_piece(arrived), by_piece(second)]
    cot_rows = by_piece(cot_arrived)
    hidden_up = jnp.einsum("erd,efd->erf", cot_rows, down_weight, preferred_element_type=f32)
    gate_pre = up_pre = slot_logits = 0.0
    for rows, span in zip(row_chunks, spans):
        gate_pre = gate_pre + jnp.einsum(
            "erd,edf->erf", rows, gate_weight[:, span], preferred_element_type=f32
        )
        up_pre = up_pre + jnp.einsum(
            "erd,edf->erf", rows, up_weight[:, span], preferred_element_type=f32
        )
        slot_logits = slot_logits + jnp.einsum(
            "erd,nd->ern", rows, router_rows[:, span], preferred_element_type=f32
        )
    slot_exp = jnp.exp(slot_logits)
    piece_ids = me_dp * pieces + jnp.arange(pieces, dtype=jnp.int32)
    mine = (piece_ids // split_count)[:, None, None] == expert_ids
    slot_gate = jnp.sum(jnp.where(mine, slot_exp, 0.0), axis=-1, keepdims=True) / jnp.sum(
        slot_exp, axis=-1, keepdims=True
    )
    activated, gelu_back = jax.vjp(gelu_tanh, gate_pre)
    hidden = (activated * up_pre).astype(bf16)
    slot_score = jnp.sum(hidden.astype(f32) * hidden_up, axis=-1)
    hidden_grad = hidden_up * slot_gate
    gate_pre_grad = gelu_back(hidden_grad * up_pre)[0].astype(bf16)
    up_pre_grad = (hidden_grad * activated).astype(bf16)

    expert_of = (piece_ids // split_count)[:, None, None]
    score_ids = jnp.arange(LANES, dtype=jnp.int32)
    score_columns = jnp.where(expert_of == score_ids, slot_score[..., None], 0.0)
    back_rows = []
    for index, span in enumerate(back_spans):
        rows_back = jnp.einsum(
            "erf,edf->erd", gate_pre_grad, gate_weight[:, span], preferred_element_type=f32
        ) + jnp.einsum("erf,edf->erd", up_pre_grad, up_weight[:, span], preferred_element_type=f32)
        rows_back = rows_back.astype(bf16)
        if index == 0:
            rows_back = jnp.concatenate([rows_back, score_columns.astype(bf16)], axis=-1)
        back_rows.append(rows_back)
    back_rows, hidden, gate_pre_grad, up_pre_grad = lax.optimization_barrier(
        (back_rows, hidden, gate_pre_grad, up_pre_grad)
    )
    out_rows = jnp.einsum("erf,efd->erd", hidden, down_weight, preferred_element_type=f32)
    out_rows = (out_rows * slot_gate).astype(bf16)
    rows_all = jnp.concatenate(row_chunks, axis=-1)
    rows_grad = (cot_rows.astype(f32) * slot_gate).astype(bf16)
    gate_grad_w = jnp.einsum("erd,erf->edf", rows_all, gate_pre_grad, preferred_element_type=f32)
    up_grad_w = jnp.einsum("erd,erf->edf", rows_all, up_pre_grad, preferred_element_type=f32)
    first_back = to_sources(by_owner(back_rows[0]))
    second_rows, first_back, gate_grad_w, up_grad_w, out_rows = together(
        by_owner(back_rows[1]), first_back, gate_grad_w, up_grad_w, by_owner(out_rows)
    )
    back_chunks = [first_back, to_sources(second_rows)]
    lows = own_parts(to_tokens(back_chunks[0]))
    last_tokens = to_tokens(back_chunks[1])
    last_tokens, out_rows, hidden_late = together(last_tokens, out_rows, hidden)
    highs = own_parts(last_tokens)
    down_grad = jnp.einsum("erf,erd->efd", hidden_late, rows_grad, preferred_element_type=f32)
    out_returned = to_sources(out_rows)

    upstream, down_grad = together(upstream, down_grad)
    input_grad, *grad_blocks = attention_backward(
        lows,
        highs,
        qkv_turned,
        gathered,
        [
            upstream, inputs, residual_one, normed_two,
            normed_turned, projected, probs, mixed_turned, small_full, turn,
        ],
    )
    out_parts = to_tokens(out_returned)
    out_tokens = sum_tokens(out_parts)
    sums = reduce_rows(grad_blocks[:2], grad_blocks[2:])
    sums = sum_groups(sums)
    block_output = residual_one + out_tokens

    base = 4 * model_width
    vector_sums = [sums[:, base + EXPERTS + i] for i in range(len(vectors))]
    return (
        block_output[None],
        input_grad[None],
        vector_sums[0],
        vector_sums[1],
        sums[:, : 3 * model_width],
        vector_sums[2],
        vector_sums[3],
        sums[:, 3 * model_width : base],
        vector_sums[4],
        vector_sums[5],
        vector_sums[6],
        sums[:, base : base + EXPERTS],
        gate_grad_w,
        up_grad_w,
        down_grad,
    )


def solution(mesh):
    in_specs = (
        P((DP, SEQ), None, None),
        P(DP),
        P(DP),
        P(DP, None),
        P(DP),
        P(DP),
        P(DP, None),
        P(DP),
        P(DP),
        P(DP),
        P(DP, None),
        P(DP, None, SEQ),
        P(DP, None, SEQ),
        P(DP, SEQ, None),
        P((DP, SEQ), None, None),
        P(DP, None),
        P((DP, SEQ), None, None),
    )
    out_specs = (
        P((DP, SEQ), None, None),
        P((DP, SEQ), None, None),
        P(DP),
        P(DP),
        P(DP, None),
        P(DP),
        P(DP),
        P(DP, None),
        P(DP),
        P(DP),
        P(DP),
        P(DP, None),
        P(DP, None, SEQ),
        P(DP, None, SEQ),
        P(DP, SEQ, None),
    )
    return jax.shard_map(
        program, mesh=mesh, in_specs=in_specs, out_specs=out_specs, check_vma=False
    )
```
